32 devices in a mesh: blk: 16 (over z, y, core), uly: 2 (over x).
Axes of the slice: x: 2, y: 2, z: 4, core: 2. Of those that a mesh axis runs over, the one named last changes fastest.
Arguments:
- queries: bfloat16 [8192, 6144], P(('blk', 'uly')), may hold values from -8 to 8
- keys: bfloat16 [2048, 6144], P(('blk', 'uly')), may hold values from -8 to 8
- values: bfloat16 [2048, 6144], P(('blk', 'uly')), may hold values from -6 to 6
- block_lists: int32 [48, 64, 16], replicated, may hold values from 0 to 15, as said below
- block_counts: int32 [48, 64], replicated, may hold values from 1 to 16, as said below
Outputs:
- attended: bfloat16 [8192, 6144], P(('blk', 'uly'))
The draws below stay inside these ranges and needn't reach their ends.
Inputs may be any that keep to these rules, and one draw needn't show every extreme that they name: `block_lists`: entry 0 of the list for query block a is always the key block at the same relative place in the sequence, the integer part of a times 16 divided by 64; the first block_counts entries of a list are distinct key blocks; entries after them are key block numbers that are ignored. `block_counts`: counts differ widely from head to head.
All inputs are finite; a program needn't handle non-finite values.
Results may differ from the reference program's by a relative error of at most 0.0055.
Values may be sent and summed in bfloat16 or wider, within the bound.
A program may use at most 256 MiB of HBM per device.

```python
import math
import jax
import jax.numpy as jnp
from jax import lax

HEADS = 48
HEAD_DIM = 128
D = 6144
BLOCK = 128
SEL_MAX = 16
QBLOCKS = 64
KBLOCKS = 16
QTOKENS = 8192
KTOKENS = 2048


def draw_queries(key, part):
    drawn = jax.random.normal(jax.random.fold_in(key, 1), (QTOKENS, D), jnp.float32)
    return jnp.clip(drawn, -8.0, 8.0).astype(jnp.bfloat16)


def draw_keys(key, part):
    drawn = jax.random.normal(jax.random.fold_in(key, 3), (KTOKENS, D), jnp.float32)
    return jnp.clip(drawn, -8.0, 8.0).astype(jnp.bfloat16)


def selection(key):
    per_head = jax.random.randint(jax.random.fold_in(key, 21), (HEADS,), 1, SEL_MAX + 1)
    jitter = jax.random.randint(jax.random.fold_in(key, 22), (HEADS, QBLOCKS), -1, 2)
    counts = jnp.clip(per_head[:, None] + jitter, 1, SEL_MAX)
    heavy = jax.random.randint(jax.random.fold_in(key, 23), (), 0, HEADS)
    counts = counts.at[heavy, 0].set(SEL_MAX)
    counts = counts.at[(heavy + 1) % HEADS, 0].set(1)
    tile_keys = jax.random.split(jax.random.fold_in(key, 24), HEADS * QBLOCKS)
    others = jax.vmap(lambda single: jax.random.permutation(single, KBLOCKS - 1)[:SEL_MAX - 1])(tile_keys)
    others = others.reshape(HEADS, QBLOCKS, SEL_MAX - 1).astype(jnp.int32)
    diagonal = (jnp.arange(QBLOCKS, dtype=jnp.int32) * KBLOCKS // QBLOCKS)[None, :, None]
    others = others + (others >= diagonal).astype(jnp.int32)
    leading = jnp.broadcast_to(diagonal, (HEADS, QBLOCKS, 1))
    lists = jnp.concatenate([leading, others], axis=2).astype(jnp.int32)
    return (lists, counts.astype(jnp.int32))


def draw_block_lists(key, part):
    return selection(key)[0]


def draw_block_counts(key, part):
    return selection(key)[1]


def steps_of(stream_key, shape, cuts, least, high):
    level = 1.0
    for axis_at, shards_of in cuts:
        heights = jax.random.uniform(jax.random.fold_in(jax.random.fold_in(stream_key, 6), axis_at), (shards_of,), jnp.float32, least / len(cuts), high / len(cuts))
        level = level * jnp.repeat(jnp.exp(heights), shape[axis_at] // shards_of).reshape((-1,) + (1,) * (len(shape) - 1 - axis_at))
    return level


def scatter_about(rng, shape, deviation, most, pieces=(), kind=jnp.bfloat16):
    entries = deviation * jax.random.normal(rng, shape, jnp.float32)
    if pieces:
        entries = entries * steps_of(rng, shape, pieces, -0.22, 0.18)
    return jnp.clip(entries, -most, most).astype(kind)


def setup_inputs(seed: int = 0) -> dict:
    key_of = jax.random.split(jax.random.key(seed), 6)
    queries = draw_queries(jax.random.fold_in(key_of[5], 71), 0)
    keys = draw_keys(jax.random.fold_in(key_of[5], 71), 0)
    values = scatter_about(key_of[2], (KTOKENS, D), 1.0, 6.0, ((0, 32),))
    block_lists = draw_block_lists(jax.random.fold_in(key_of[5], 71), 0)
    block_counts = draw_block_counts(jax.random.fold_in(key_of[5], 71), 0)
    return {"queries": queries, "keys": keys, "values": values, "block_lists": block_lists, "block_counts": block_counts}


NEGATIVE = -1e+30

def reference(queries, keys, values, block_lists, block_counts):
    scaling = 1.0 / math.sqrt(HEAD_DIM)

    def one_tile(position):
        head_index = position // QBLOCKS
        query_block = position % QBLOCKS
        query_rows = lax.dynamic_slice(queries, (query_block * BLOCK, head_index * HEAD_DIM), (BLOCK, HEAD_DIM)).astype(jnp.float32)
        listed = block_lists[head_index, query_block]
        count_used = block_counts[head_index, query_block]

        def fetch(block_number):
            first = (block_number * BLOCK).astype(jnp.int32)
            column = (head_index * HEAD_DIM).astype(jnp.int32)
            key_tile = lax.dynamic_slice(keys, (first, column), (BLOCK, HEAD_DIM))
            value_tile = lax.dynamic_slice(values, (first, column), (BLOCK, HEAD_DIM))
            return (key_tile, value_tile)
        key_tiles, value_tiles = jax.vmap(fetch)(listed)
        key_flat = key_tiles.reshape(SEL_MAX * BLOCK, HEAD_DIM).astype(jnp.float32)
        value_flat = value_tiles.reshape(SEL_MAX * BLOCK, HEAD_DIM).astype(jnp.float32)
        scores = jnp.einsum('qd,kd->qk', query_rows, key_flat) * scaling
        usable = jnp.repeat(jnp.arange(SEL_MAX, dtype=jnp.int32) < count_used, BLOCK)[None, :]
        top = lax.optimization_barrier(jnp.max(jnp.where(usable, scores, NEGATIVE), axis=1))
        weights = jnp.where(usable, jnp.exp(scores - top[:, None]), 0.0)
        total = lax.optimization_barrier(jnp.sum(weights, axis=1))
        rounded = lax.optimization_barrier(weights.astype(jnp.bfloat16)).astype(jnp.float32)
        mixed = jnp.einsum('qk,kd->qd', rounded, value_flat) / total[:, None]
        return mixed.astype(jnp.bfloat16)
    tiles = lax.map(one_tile, jnp.arange(HEADS * QBLOCKS, dtype=jnp.int32))
    tiles = tiles.reshape(HEADS, QBLOCKS * BLOCK, HEAD_DIM)
    return jnp.transpose(tiles, (1, 0, 2)).reshape(QBLOCKS * BLOCK, HEADS * HEAD_DIM)
```

```python
import functools
import math

import jax
import jax.numpy as jnp
from jax import lax
from jax.experimental import pallas as pl
from jax.experimental.pallas import tpu as pltpu
from jax.sharding import PartitionSpec as P

HEAD_DIM = 128
BLOCK = 128
NEGATIVE = -1e30
MESH = pl.DeviceIdType.MESH


def mix(a, b, n):
    if n & (n - 1):
        return lax.rem(n + b - a, n)
    out, bit = 0, 1
    while bit < n:
        out = out + lax.rem(a // bit + b // bit, 2) * bit
        bit *= 2
    return out


def attend_kernel(
    blk_n, uly_n, group, q_any, k_any, v_any, bias_ref, o_any,
    qbuf, kbuf, vbuf, obuf, hot,
    kv_send, k_recv, v_recv, q_send, q_recv, o_send, o_recv, local_sem,
):
    devices = blk_n * uly_n
    me = lax.axis_index("blk") * uly_n + lax.axis_index("uly")
    first = (me // group) * group
    place = me - first
    rows = q_any.shape[0]
    width = qbuf.shape[2]
    heads = width // HEAD_DIM
    keys_all = kbuf.shape[0] * kbuf.shape[1]
    flags = bias_ref.shape[2]
    scaling = math.log2(math.e) / math.sqrt(HEAD_DIM)

    def coords(device):
        return (device // uly_n, lax.rem(device, uly_n))

    def columns(position):
        return pl.ds(pl.multiple_of(position * width, HEAD_DIM), width)

    own = (
        pltpu.make_async_copy(k_any.at[:, columns(place)], kbuf.at[me], local_sem.at[0]),
        pltpu.make_async_copy(v_any.at[:, columns(place)], vbuf.at[me], local_sem.at[1]),
        pltpu.make_async_copy(q_any.at[:, columns(place)], qbuf.at[place], local_sem.at[2]),
    )
    for copy in own:
        copy.start()

    barrier = pltpu.get_barrier_semaphore()

    def greet(step, carry):
        other = lax.rem(me + step, devices)
        pl.semaphore_signal(barrier, inc=1, device_id=coords(other), device_id_type=MESH)
        return carry

    lax.fori_loop(1, devices, greet, 0)
    pl.semaphore_wait(barrier, devices - 1)

    def send_kv(step, carry):
        other = mix(me, step, devices)
        cols = columns(lax.rem(other, group))
        pltpu.make_async_remote_copy(
            src_ref=k_any.at[:, cols], dst_ref=kbuf.at[me],
            send_sem=kv_send.at[0], recv_sem=k_recv,
            device_id=coords(other), device_id_type=MESH,
        ).start()
        pltpu.make_async_remote_copy(
            src_ref=v_any.at[:, cols], dst_ref=vbuf.at[me],
            send_sem=kv_send.at[1], recv_sem=v_recv,
            device_id=coords(other), device_id_type=MESH,
        ).start()
        return carry

    lax.fori_loop(1, devices, send_kv, 0)

    def send_q(step, carry):
        there = mix(place, step, group)
        pltpu.make_async_remote_copy(
            src_ref=q_any.at[:, columns(there)], dst_ref=qbuf.at[place],
            send_sem=q_send, recv_sem=q_recv.at[place],
            device_id=coords(first + there), device_id_type=MESH,
        ).start()
        return carry

    lax.fori_loop(1, group, send_q, 0)

    key_block = lax.broadcasted_iota(jnp.int32, hot.shape, 0) // BLOCK
    lane = lax.broadcasted_iota(jnp.int32, hot.shape, 1)
    hot[...] = jnp.where(key_block == lane, 1.0, 0.0).astype(jnp.bfloat16)

    for copy in own:
        copy.wait()
    rest = pl.ds(0, devices - 1)
    pltpu.make_async_copy(kbuf.at[rest], kbuf.at[rest], k_recv).wait()
    pltpu.make_async_copy(vbuf.at[rest], vbuf.at[rest], v_recv).wait()

    def attend(source):
        for head in range(heads):
            cols = slice(head * HEAD_DIM, (head + 1) * HEAD_DIM)
            spans = max(rows // BLOCK, 1)
            flag = [
                jnp.broadcast_to(
                    bias_ref[head, pl.ds((source * rows) // BLOCK + b, 1), :],
                    (rows // spans, flags),
                ).astype(jnp.bfloat16)
                for b in range(spans)
            ]
            query = jnp.concatenate([qbuf[source, :, cols], jnp.concatenate(flag, axis=0)], axis=1)
            key = jnp.concatenate(
                [kbuf[:, :, cols].reshape(keys_all, HEAD_DIM), hot[...]], axis=1
            )
            value = vbuf[:, :, cols].reshape(keys_all, HEAD_DIM)
            scores = lax.dot_general(
                query, key, (((1,), (1,)), ((), ())), preferred_element_type=jnp.float32
            )
            top = jnp.max(scores, axis=1, keepdims=True)
            weights = jnp.exp2((scores - top) * scaling)
            total = jnp.sum(weights, axis=1, keepdims=True)
            mixed = jnp.dot(
                weights.astype(jnp.bfloat16), value, preferred_element_type=jnp.float32
            )
            obuf[source, :, cols] = (mixed / total).astype(jnp.bfloat16)

    attend(place)
    home = pltpu.make_async_copy(
        obuf.at[place], o_any.at[:, columns(place)], local_sem.at[3]
    )
    home.start()

    def visit(step, carry):
        source = mix(place, step, group)
        pltpu.make_async_copy(qbuf.at[source], qbuf.at[source], q_recv.at[source]).wait()
        attend(source)
        pltpu.make_async_remote_copy(
            src_ref=obuf.at[source], dst_ref=o_any.at[:, columns(place)],
            send_sem=o_send, recv_sem=o_recv,
            device_id=coords(first + source), device_id_type=MESH,
        ).start()
        return carry

    lax.fori_loop(1, group, visit, 0)
    home.wait()
    pltpu.make_async_copy(kbuf.at[rest], kbuf.at[rest], kv_send.at[0]).wait()
    pltpu.make_async_copy(vbuf.at[rest], vbuf.at[rest], kv_send.at[1]).wait()
    peers = pl.ds(0, group - 1)
    pltpu.make_async_copy(qbuf.at[peers], qbuf.at[peers], q_send).wait()
    pltpu.make_async_copy(obuf.at[peers], obuf.at[peers], o_send).wait()
    pltpu.make_async_copy(obuf.at[peers], obuf.at[peers], o_recv).wait()


def line_kernel(
    planes, per_blk, uly_n, q_any, k_any, v_any, bias_ref, o_any,
    qbuf, kbuf, vbuf, obuf, hot,
    k_in, v_in, q_in, k_line, v_line, far_in,
    flat_send, line_send, far_send, o_send, o_recv, o_home,
):
    side = per_blk * uly_n
    blk, uly = lax.axis_index("blk"), lax.axis_index("uly")
    z = blk // per_blk
    place = lax.rem(blk, per_blk) * uly_n + uly
    partner = z + 1 - 2 * lax.rem(z, 2)
    across = planes - 1 - z
    beyond = across + 1 - 2 * lax.rem(across, 2)
    edge = (z + 1) // planes + (planes - z) // planes
    is_edge, is_mid = edge == 1, edge == 0
    rows, key_rows = q_any.shape[0], k_any.shape[0]
    heads = kbuf.shape[0]
    far = heads // 2
    near = heads - far
    keys_all = kbuf.shape[1] * kbuf.shape[2]
    flags = bias_ref.shape[2]
    scaling = math.log2(math.e) / math.sqrt(HEAD_DIM)
    spans = rows // BLOCK

    def coords(plane, position):
        return (plane * per_blk + position // uly_n, lax.rem(position, uly_n))

    def columns(position, j):
        return pl.ds(pl.multiple_of((position * heads + j) * HEAD_DIM, HEAD_DIM), HEAD_DIM)

    def remote(src, dst, send, recv, plane, position):
        pltpu.make_async_remote_copy(
            src_ref=src, dst_ref=dst, send_sem=send, recv_sem=recv,
            device_id=coords(plane, position), device_id_type=MESH,
        ).start()

    def drain(ref, sem):
        pltpu.make_async_copy(ref, ref, sem).wait()

    mine = pl.ds(pl.multiple_of(place * key_rows, key_rows), key_rows)
    for j in range(heads):
        cols = columns(place, j)
        pltpu.make_async_copy(k_any.at[:, cols], kbuf.at[j, z, mine], k_in.at[j]).start()
        pltpu.make_async_copy(v_any.at[:, cols], vbuf.at[j, z, mine], v_in.at[j]).start()
        pltpu.make_async_copy(q_any.at[:, cols], qbuf.at[j, place], q_in.at[j]).start()

    barrier = pltpu.get_barrier_semaphore()

    def greet(plane, first):
        def signal(step, carry):
            other = coords(plane, mix(place, step, side))
            pl.semaphore_signal(barrier, inc=1, device_id=other, device_id_type=MESH)
            return carry

        lax.fori_loop(first, side, signal, 0)

    greet(z, 1)
    greet(partner, 0)

    @pl.when(is_mid)
    def _():
        pl.semaphore_signal(barrier, inc=1, device_id=coords(across, place), device_id_type=MESH)

    pl.semaphore_wait(barrier, 2 * side - edge)

    def send_kv(j):
        def body(step, carry):
            other = mix(place, step, side)
            cols = columns(other, j)
            remote(k_any.at[:, cols], kbuf.at[j, z, mine], flat_send.at[0], k_in.at[j], z, other)
            remote(v_any.at[:, cols], vbuf.at[j, z, mine], flat_send.at[1], v_in.at[j], z, other)
            return carry

        lax.fori_loop(1, side, body, 0)

    def send_q(j):
        def body(step, carry):
            other = mix(place, step, side)
            cols = columns(other, j)
            remote(q_any.at[:, cols], qbuf.at[j, place], flat_send.at[2], q_in.at[j], z, other)
            return carry

        lax.fori_loop(1, side, body, 0)

    def hand(j, block, plane, way):
        for buf, sem, arrived in ((kbuf, line_send.at[way, 0], k_line), (vbuf, line_send.at[way, 1], v_line)):
            remote(buf.at[j, block], buf.at[j, block], sem, arrived.at[j, block], plane, place)

    def arrive(j, block):
        drain(kbuf.at[j, block], k_line.at[j, block])
        drain(vbuf.at[j, block], v_line.at[j, block])

    def gathered(j):
        drain(kbuf.at[j, z], k_in.at[j])
        drain(vbuf.at[j, z], v_in.at[j])

    def edge_own(j):
        gathered(j)
        hand(j, z, partner, 1)

    def edge_queries(j):
        drain(qbuf.at[j], q_in.at[j])
        remote(qbuf.at[j], qbuf.at[heads + j // 2], far_send, far_in.at[j // 2], partner, place)

    def edge_ready(j):
        for block in (partner, beyond, across):
            arrive(j, block)
        drain(qbuf.at[j], q_in.at[j])

    def mid_own(j):
        gathered(j)
        hand(j, z, across, 0)
        if j % 2 == 0:
            hand(j, z, partner, 1)

    def mid_outer(j):
        arrive(j, partner)
        hand(j, partner, across, 0)

    def mid_inner(j):
        for block in (across, beyond):
            arrive(j, block)
            if j % 2 == 0:
                hand(j, block, partner, 1)

    def mid_queries(j):
        drain(qbuf.at[j], q_in.at[j])

    def mid_far(j):
        drain(qbuf.at[heads + j // 2], far_in.at[j // 2])

    def own(j):
        pl.when(is_edge)(lambda: edge_own(j))
        pl.when(is_mid)(lambda: mid_own(j))

    send_kv(0)
    send_kv(1)
    send_q(0)
    key_block = lax.broadcasted_iota(jnp.int32, hot.shape, 0) // BLOCK
    lane = lax.broadcasted_iota(jnp.int32, hot.shape, 1)
    hot[...] = jnp.where(key_block == lane, 1.0, 0.0).astype(jnp.bfloat16)
    own(0)
    for j in range(2, heads):
        send_kv(j)
        send_q(j - 1)
        if j == 3:
            own(1)
    send_q(heads - 1)

    @pl.when(is_mid)
    def _():
        mid_outer(0)
        mid_own(2)

    @pl.when(is_edge)
    def _():
        edge_own(2)
        edge_queries(1)
        edge_own(3)

    def mid_before(g):
        t, r = divmod(g, 3)
        is_far = r == (1 if t == far - 1 else 2)
        j = 2 * t + (r > 0)
        for i in range(*upto(own_done, g)):
            mid_own(i)
        for i in range(*upto(outer_done, g)):
            mid_outer(i)
        for i in range(*upto(inner_done, g)):
            mid_inner(i)
        if is_far:
            mid_far(j)
        else:
            mid_queries(j)

    def upto(done, g):
        return done[g], done[g + 1]

    groups = 3 * far
    own_done = [3] + [min(heads, 3 + g) for g in range(groups)]
    outer_done = [1] + [
        min(heads, 2 * (g // 3) + 2 + (g % 3 > 0) * (1 + (g >= 3))) for g in range(groups)
    ]
    inner_done = [0] + [
        min(heads, 2 * (g // 3) + 1 + (g % 3 > 0) + (g % 3 == 2 and g >= 3)) for g in range(groups)
    ]

    def edge_before(g):
        if g == 1:
            for j in range(4, heads):
                edge_own(j)
            for j in range(3, heads, 2):
                edge_queries(j)
        edge_ready(2 * g)

    def attend(source, slot, j, plane):
        flag = [
            jnp.broadcast_to(
                bias_ref[j, pl.ds((plane * side + source) * spans + b, 1), :], (BLOCK, flags)
            ).astype(jnp.bfloat16)
            for b in range(spans)
        ]
        query = jnp.concatenate([qbuf[slot, source], jnp.concatenate(flag, axis=0)], axis=1)
        key = jnp.concatenate([kbuf[j].reshape(keys_all, HEAD_DIM), hot[...]], axis=1)
        value = vbuf[j].reshape(keys_all, HEAD_DIM)
        scores = lax.dot_general(
            query, key, (((1,), (1,)), ((), ())), preferred_element_type=jnp.float32
        )
        top = jnp.max(scores, axis=1, keepdims=True)
        weights = jnp.exp2((scores - top) * scaling)
        total = jnp.sum(weights, axis=1, keepdims=True)
        mixed = jnp.dot(
            weights.astype(jnp.bfloat16), value, preferred_element_type=jnp.float32
        )
        obuf[slot, source] = (mixed / total).astype(jnp.bfloat16)

    def group(g, carry):
        for k in range(groups):
            pl.when(jnp.logical_and(is_mid, g == k))(functools.partial(mid_before, k))
        for k in range(near):
            pl.when(jnp.logical_and(is_edge, g == k))(functools.partial(edge_before, k))
        t, r = g // 3, lax.rem(g, 3)
        last = t // (far - 1)
        is_far = (1 - edge) * ((r // 2) * (1 - last) + lax.rem(r, 2) * last)
        j = edge * 2 * g + (1 - edge) * (2 * t + (r + 1) // 2)
        slot = j + is_far * (heads + j // 2 - j)
        plane = z + is_far * (partner - z)
        cols = columns(place, j)

        def visit(step, carry):
            source = mix(place, lax.rem(step, side), side)
            attend(source, slot, j, plane)
            at_home = jnp.logical_and(is_far == 0, step == side)

            @pl.when(at_home)
            def _():
                pltpu.make_async_copy(obuf.at[slot, source], o_any.at[:, cols], o_home).start()

            @pl.when(jnp.logical_not(at_home))
            def _():
                remote(
                    obuf.at[slot, source], o_any.at[:, cols],
                    o_send.at[is_far], o_recv.at[is_far], plane, source,
                )

            return carry

        return lax.fori_loop(1, side + 1, visit, carry)

    lax.fori_loop(0, edge * near + (1 - edge) * groups, group, 0)

    others = pl.ds(0, side - 1)
    drain(kbuf.at[:, 0, pl.ds(0, (side - 1) * key_rows)], flat_send.at[0])
    drain(vbuf.at[:, 0, pl.ds(0, (side - 1) * key_rows)], flat_send.at[1])
    drain(qbuf.at[pl.ds(0, heads), others], flat_send.at[2])

    @pl.when(is_mid)
    def _():
        for i, buf in enumerate((kbuf, vbuf)):
            drain(buf.at[:, pl.ds(0, 2)], line_send.at[0, i])
            drain(buf.at[pl.ds(0, near), pl.ds(0, 3)], line_send.at[1, i])
        drain(obuf.at[pl.ds(0, heads), 0], o_home)
        drain(obuf.at[pl.ds(0, heads), others], o_send.at[0])
        drain(obuf.at[pl.ds(0, far)], o_send.at[1])
        drain(obuf.at[pl.ds(0, heads), others], o_recv.at[0])

    @pl.when(is_edge)
    def _():
        for i, buf in enumerate((kbuf, vbuf)):
            drain(buf.at[:, 0], line_send.at[1, i])
        drain(qbuf.at[pl.ds(0, far)], far_send)
        drain(obuf.at[pl.ds(0, near), 0], o_home)
        drain(obuf.at[pl.ds(0, near), others], o_send.at[0])
        drain(obuf.at[pl.ds(0, near), others], o_recv.at[0])
        drain(obuf.at[pl.ds(0, far)], o_recv.at[1])


def flagged(lists, counts, key_blocks):
    listed = lists.shape[2]
    usable = jnp.arange(listed, dtype=jnp.int32) < counts[:, :, None]
    chosen = jnp.where(usable, lists, -1)
    flags = -(-key_blocks // HEAD_DIM) * HEAD_DIM
    blocks = jnp.arange(flags, dtype=jnp.int32)
    member = jnp.any(chosen[:, :, :, None] == blocks, axis=2)
    return jnp.where(member, 0.0, NEGATIVE).astype(jnp.float32)


LINE = 4
CORES = 2


def fits_line(blk_n, uly_n, heads_all, rows):
    per_blk = blk_n // LINE
    side = per_blk * uly_n
    return (
        blk_n % LINE == 0 and uly_n == CORES and per_blk == 2 * CORES
        and heads_all % side == 0 and (heads_all // side) % 2 == 0 and heads_all // side >= 4
        and rows % BLOCK == 0
    )


def along_line(blk_n, uly_n, queries, keys, values, block_lists, block_counts):
    heads_all, qblocks_all, listed = block_lists.shape
    devices, planes = blk_n * uly_n, LINE
    per_blk = blk_n // planes
    side = per_blk * uly_n
    heads = heads_all // side
    slots = heads + heads // 2
    rows, key_rows = queries.shape[0], keys.shape[0]
    keys_all = key_rows * devices

    place = lax.rem(lax.axis_index("blk"), per_blk) * uly_n + lax.axis_index("uly")
    lists = lax.dynamic_slice_in_dim(block_lists, place * heads, heads, 0)
    counts = lax.dynamic_slice_in_dim(block_counts, place * heads, heads, 0)
    bias = flagged(lists, counts, keys_all // BLOCK)

    any_spec = pl.BlockSpec(memory_space=pl.ANY)
    dma = pltpu.SemaphoreType.DMA
    plane_keys = side * key_rows
    return pl.pallas_call(
        functools.partial(line_kernel, planes, per_blk, uly_n),
        out_shape=jax.ShapeDtypeStruct(queries.shape, queries.dtype),
        in_specs=[any_spec, any_spec, any_spec, pl.BlockSpec(memory_space=pltpu.VMEM)],
        out_specs=any_spec,
        scratch_shapes=[
            pltpu.VMEM((slots, side, rows, HEAD_DIM), jnp.bfloat16),
            pltpu.VMEM((heads, planes, plane_keys, HEAD_DIM), jnp.bfloat16),
            pltpu.VMEM((heads, planes, plane_keys, HEAD_DIM), jnp.bfloat16),
            pltpu.VMEM((slots, side, rows, HEAD_DIM), jnp.bfloat16),
            pltpu.VMEM((keys_all, bias.shape[2]), jnp.bfloat16),
            dma((heads,)), dma((heads,)), dma((heads,)),
            dma((heads, planes)), dma((heads, planes)), dma((heads // 2,)),
            dma((3,)), dma((2, 2)), dma, dma((2,)), dma((2,)), dma,
        ],
        compiler_params=pltpu.CompilerParams(
            collective_id=1, has_side_effects=True, vmem_limit_bytes=60 * 1024 * 1024
        ),
    )(queries, keys, values, bias)


def local(blk_n, uly_n, queries, keys, values, block_lists, block_counts):
    heads_all, qblocks_all, listed = block_lists.shape
    if fits_line(blk_n, uly_n, heads_all, queries.shape[0]):
        return along_line(blk_n, uly_n, queries, keys, values, block_lists, block_counts)
    share = math.gcd(blk_n, heads_all // uly_n)
    group = share * uly_n
    heads = heads_all // group
    groups = blk_n // share
    qblocks = qblocks_all // groups
    devices = blk_n * uly_n
    rows, key_rows = queries.shape[0], keys.shape[0]
    width = heads * HEAD_DIM
    keys_all = key_rows * devices

    me = lax.axis_index("blk") * uly_n + lax.axis_index("uly")
    place = lax.rem(me, group)
    lists = lax.dynamic_slice(
        block_lists, (place * heads, (me // group) * qblocks, 0), (heads, qblocks, listed)
    )
    counts = lax.dynamic_slice(
        block_counts, (place * heads, (me // group) * qblocks), (heads, qblocks)
    )
    bias = flagged(lists, counts, keys_all // BLOCK)
    flags = bias.shape[2]

    any_spec = pl.BlockSpec(memory_space=pl.ANY)
    dma = pltpu.SemaphoreType.DMA
    return pl.pallas_call(
        functools.partial(attend_kernel, blk_n, uly_n, group),
        out_shape=jax.ShapeDtypeStruct(queries.shape, queries.dtype),
        in_specs=[any_spec, any_spec, any_spec, pl.BlockSpec(memory_space=pltpu.VMEM)],
        out_specs=any_spec,
        scratch_shapes=[
            pltpu.VMEM((group, rows, width), jnp.bfloat16),
            pltpu.VMEM((devices, key_rows, width), jnp.bfloat16),
            pltpu.VMEM((devices, key_rows, width), jnp.bfloat16),
            pltpu.VMEM((group, rows, width), jnp.bfloat16),
            pltpu.VMEM((keys_all, flags), jnp.bfloat16),
            dma((2,)), dma, dma, dma, dma((group,)), dma, dma, dma((4,)),
        ],
        compiler_params=pltpu.CompilerParams(
            collective_id=0, has_side_effects=True, vmem_limit_bytes=60 * 1024 * 1024
        ),
    )(queries, keys, values, bias)


def solution(mesh):
    return jax.shard_map(
        functools.partial(local, mesh.shape["blk"], mesh.shape["uly"]),
        mesh=mesh,
        in_specs=(
            P(("blk", "uly"), None),
            P(("blk", "uly"), None),
            P(("blk", "uly"), None),
            P(),
            P(),
        ),
        out_specs=P(("blk", "uly"), None),
        check_vma=False,
    )
```

```python
import functools
import math

import jax
import jax.numpy as jnp
from jax import lax
from jax.experimental import pallas as pl
from jax.experimental.pallas import tpu as pltpu
from jax.sharding import PartitionSpec as P

HEAD_DIM = 128
BLOCK = 128
NEGATIVE = -1e30
MESH = pl.DeviceIdType.MESH


def mix(a, b, n):
    if n & (n - 1):
        return lax.rem(n + b - a, n)
    out, bit = 0, 1
    while bit < n:
        out = out + lax.rem(a // bit + b // bit, 2) * bit
        bit *= 2
    return out


def attend_kernel(
    blk_n, uly_n, group, q_any, k_any, v_any, bias_ref, o_any,
    qbuf, kbuf, vbuf, obuf, hot,
    kv_send, k_recv, v_recv, q_send, q_recv, o_send, o_recv, local_sem,
):
    devices = blk_n * uly_n
    me = lax.axis_index("blk") * uly_n + lax.axis_index("uly")
    first = (me // group) * group
    place = me - first
    rows = q_any.shape[0]
    width = qbuf.shape[2]
    heads = width // HEAD_DIM
    keys_all = kbuf.shape[0] * kbuf.shape[1]
    flags = bias_ref.shape[2]
    scaling = math.log2(math.e) / math.sqrt(HEAD_DIM)

    def coords(device):
        return (device // uly_n, lax.rem(device, uly_n))

    def columns(position):
        return pl.ds(pl.multiple_of(position * width, HEAD_DIM), width)

    own = (
        pltpu.make_async_copy(k_any.at[:, columns(place)], kbuf.at[me], local_sem.at[0]),
        pltpu.make_async_copy(v_any.at[:, columns(place)], vbuf.at[me], local_sem.at[1]),
        pltpu.make_async_copy(q_any.at[:, columns(place)], qbuf.at[place], local_sem.at[2]),
    )
    for copy in own:
        copy.start()

    barrier = pltpu.get_barrier_semaphore()

    def greet(step, carry):
        other = lax.rem(me + step, devices)
        pl.semaphore_signal(barrier, inc=1, device_id=coords(other), device_id_type=MESH)
        return carry

    lax.fori_loop(1, devices, greet, 0)
    pl.semaphore_wait(barrier, devices - 1)

    def send_kv(step, carry):
        other = mix(me, step, devices)
        cols = columns(lax.rem(other, group))
        pltpu.make_async_remote_copy(
            src_ref=k_any.at[:, cols], dst_ref=kbuf.at[me],
            send_sem=kv_send.at[0], recv_sem=k_recv,
            device_id=coords(other), device_id_type=MESH,
        ).start()
        pltpu.make_async_remote_copy(
            src_ref=v_any.at[:, cols], dst_ref=vbuf.at[me],
            send_sem=kv_send.at[1], recv_sem=v_recv,
            device_id=coords(other), device_id_type=MESH,
        ).start()
        return carry

    lax.fori_loop(1, devices, send_kv, 0)

    def send_q(step, carry):
        there = mix(place, step, group)
        pltpu.make_async_remote_copy(
            src_ref=q_any.at[:, columns(there)], dst_ref=qbuf.at[place],
            send_sem=q_send, recv_sem=q_recv.at[place],
            device_id=coords(first + there), device_id_type=MESH,
        ).start()
        return carry

    lax.fori_loop(1, group, send_q, 0)

    key_block = lax.broadcasted_iota(jnp.int32, hot.shape, 0) // BLOCK
    lane = lax.broadcasted_iota(jnp.int32, hot.shape, 1)
    hot[...] = jnp.where(key_block == lane, 1.0, 0.0).astype(jnp.bfloat16)

    for copy in own:
        copy.wait()
    rest = pl.ds(0, devices - 1)
    pltpu.make_async_copy(kbuf.at[rest], kbuf.at[rest], k_recv).wait()
    pltpu.make_async_copy(vbuf.at[rest], vbuf.at[rest], v_recv).wait()

    def attend(source):
        for head in range(heads):
            cols = slice(head * HEAD_DIM, (head + 1) * HEAD_DIM)
            spans = max(rows // BLOCK, 1)
            flag = [
                jnp.broadcast_to(
                    bias_ref[head, pl.ds((source * rows) // BLOCK + b, 1), :],
                    (rows // spans, flags),
                ).astype(jnp.bfloat16)
                for b in range(spans)
            ]
            query = jnp.concatenate([qbuf[source, :, cols], jnp.concatenate(flag, axis=0)], axis=1)
            key = jnp.concatenate(
                [kbuf[:, :, cols].reshape(keys_all, HEAD_DIM), hot[...]], axis=1
            )
            value = vbuf[:, :, cols].reshape(keys_all, HEAD_DIM)
            scores = lax.dot_general(
                query, key, (((1,), (1,)), ((), ())), preferred_element_type=jnp.float32
            )
            top = jnp.max(scores, axis=1, keepdims=True)
            weights = jnp.exp2((scores - top) * scaling)
            total = jnp.sum(weights, axis=1, keepdims=True)
            mixed = jnp.dot(
                weights.astype(jnp.bfloat16), value, preferred_element_type=jnp.float32
            )
            obuf[source, :, cols] = (mixed / total).astype(jnp.bfloat16)

    attend(place)
    home = pltpu.make_async_copy(
        obuf.at[place], o_any.at[:, columns(place)], local_sem.at[3]
    )
    home.start()

    def visit(step, carry):
        source = mix(place, step, group)
        pltpu.make_async_copy(qbuf.at[source], qbuf.at[source], q_recv.at[source]).wait()
        attend(source)
        pltpu.make_async_remote_copy(
            src_ref=obuf.at[source], dst_ref=o_any.at[:, columns(place)],
            send_sem=o_send, recv_sem=o_recv,
            device_id=coords(first + source), device_id_type=MESH,
        ).start()
        return carry

    lax.fori_loop(1, group, visit, 0)
    home.wait()
    pltpu.make_async_copy(kbuf.at[rest], kbuf.at[rest], kv_send.at[0]).wait()
    pltpu.make_async_copy(vbuf.at[rest], vbuf.at[rest], kv_send.at[1]).wait()
    peers = pl.ds(0, group - 1)
    pltpu.make_async_copy(qbuf.at[peers], qbuf.at[peers], q_send).wait()
    pltpu.make_async_copy(obuf.at[peers], obuf.at[peers], o_send).wait()
    pltpu.make_async_copy(obuf.at[peers], obuf.at[peers], o_recv).wait()


def pick(index, entries):
    value, n = entries[0], len(entries)
    for at in range(1, n):
        value = value + (entries[at] - entries[at - 1]) * ((index - at + n) // n)
    return value


def line_kernel(
    planes, per_blk, uly_n, q_any, k_any, v_any, lists_any, counts_any, o_any,
    qbuf, kbuf, vbuf, obuf, hot, bias, listed, counted, scores, tops,
    k_in, v_in, q_in, k_line, v_line, far_in,
    flat_send, line_send, far_send, o_send, o_recv, o_home, list_in,
):
    side = per_blk * uly_n
    blk, uly = lax.axis_index("blk"), lax.axis_index("uly")
    z = blk // per_blk
    place = lax.rem(blk, per_blk) * uly_n + uly
    partner = z + 1 - 2 * lax.rem(z, 2)
    across = planes - 1 - z
    beyond = across + 1 - 2 * lax.rem(across, 2)
    edge = (z + 1) // planes + (planes - z) // planes
    is_edge, is_mid = edge == 1, edge == 0
    rows, key_rows = q_any.shape[0], k_any.shape[0]
    heads = kbuf.shape[0]
    shared = shared_heads(heads)
    kept = [j for j in range(heads) if j not in shared]
    far, near = len(shared), len(kept)
    plane_keys = kbuf.shape[2]
    keys_all = planes * plane_keys
    flags = bias.shape[2]
    scaling = math.log2(math.e) / math.sqrt(HEAD_DIM)
    spans = rows // BLOCK

    def coords(plane, position):
        return (plane * per_blk + position // uly_n, lax.rem(position, uly_n))

    def columns(position, j):
        return pl.ds(pl.multiple_of((position * heads + j) * HEAD_DIM, HEAD_DIM), HEAD_DIM)

    def remote(src, dst, send, recv, plane, position):
        pltpu.make_async_remote_copy(
            src_ref=src, dst_ref=dst, send_sem=send, recv_sem=recv,
            device_id=coords(plane, position), device_id_type=MESH,
        ).start()

    def drain(ref, sem):
        pltpu.make_async_copy(ref, ref, sem).wait()

    mine = pl.ds(pl.multiple_of(place * key_rows, key_rows), key_rows)

    barrier = pltpu.get_barrier_semaphore()

    def greet(plane, first):
        def signal(step, carry):
            other = coords(plane, mix(place, step, side))
            pl.semaphore_signal(barrier, inc=1, device_id=other, device_id_type=MESH)
            return carry

        lax.fori_loop(first, side, signal, 0)

    greet(z, 1)
    greet(partner, 0)

    @pl.when(is_mid)
    def _():
        pl.semaphore_signal(barrier, inc=1, device_id=coords(across, place), device_id_type=MESH)

    own_lists = pltpu.make_async_copy(lists_any.at[pl.ds(place * heads, heads)], listed, list_in.at[0])
    all_counts = pltpu.make_async_copy(counts_any, counted, list_in.at[1])
    own_lists.start()
    all_counts.start()
    for j in range(heads):
        cols = columns(place, j)
        pltpu.make_async_copy(k_any.at[:, cols], kbuf.at[j, z, mine], k_in.at[j]).start()
        pltpu.make_async_copy(v_any.at[:, cols], vbuf.at[j, z, mine], v_in.at[j]).start()
        pltpu.make_async_copy(q_any.at[:, cols], qbuf.at[j, place], q_in.at[j]).start()

    pl.semaphore_wait(barrier, 2 * side - edge)

    def send_kv(j):
        def body(step, carry):
            other = mix(place, step, side)
            cols = columns(other, j)
            remote(k_any.at[:, cols], kbuf.at[j, z, mine], flat_send.at[0], k_in.at[j], z, other)
            remote(v_any.at[:, cols], vbuf.at[j, z, mine], flat_send.at[1], v_in.at[j], z, other)
            return carry

        lax.fori_loop(1, side, body, 0)

    def send_q(j):
        def body(step, carry):
            other = mix(place, step, side)
            cols = columns(other, j)
            remote(q_any.at[:, cols], qbuf.at[j, place], flat_send.at[2], q_in.at[j], z, other)
            return carry

        lax.fori_loop(1, side, body, 0)

    def hand(j, block, plane, way):
        for buf, sem, arrived in ((kbuf, line_send.at[way, 0], k_line), (vbuf, line_send.at[way, 1], v_line)):
            remote(buf.at[j, block], buf.at[j, block], sem, arrived.at[j, block], plane, place)

    def arrive(j, block):
        drain(kbuf.at[j, block], k_line.at[j, block])
        drain(vbuf.at[j, block], v_line.at[j, block])

    def queries(j):
        drain(qbuf.at[j], q_in.at[j])

    def edge_own(j):
        drain(kbuf.at[j, z], k_in.at[j])
        drain(vbuf.at[j, z], v_in.at[j])
        hand(j, z, partner, 1)

    def edge_queries(j):
        queries(j)
        at = shared.index(j)
        remote(qbuf.at[j], qbuf.at[heads + at], far_send, far_in.at[at], partner, place)

    def edge_ready(j):
        for block in (partner, beyond, across):
            arrive(j, block)
        queries(j)

    def mid_own(j):
        drain(kbuf.at[j, z], k_in.at[j])
        drain(vbuf.at[j, z], v_in.at[j])
        hand(j, z, across, 0)
        if j in kept:
            hand(j, z, partner, 1)

    def mid_outer(j):
        arrive(j, partner)
        hand(j, partner, across, 0)

    def mid_inner(j):
        for block in (across, beyond):
            arrive(j, block)
            if j in kept:
                hand(j, block, partner, 1)

    def mid_far(j):
        at = shared.index(j)
        drain(qbuf.at[heads + at], far_in.at[at])

    order = ["kv0", "kv1", "q0", "own0", "kv2", "q2", "own1"]
    for j in range(3, heads):
        order.append("kv%d" % j)
        if j == 3:
            order.append("q1")
        elif j in shared:
            order.append("q%d" % j)
    order += ["q%d" % j for j in range(heads) if "q%d" % j not in order]
    for what in order:
        j = int(what.lstrip("kvqown"))
        if what.startswith("kv"):
            send_kv(j)
        elif what.startswith("q"):
            send_q(j)
        else:
            pl.when(is_edge)(functools.partial(edge_own, j))
            pl.when(is_mid)(functools.partial(mid_own, j))

    key_block = lax.broadcasted_iota(jnp.int32, hot.shape, 0) // BLOCK
    lane = lax.broadcasted_iota(jnp.int32, hot.shape, 1)
    hot[...] = jnp.where(key_block == lane, 1.0, 0.0).astype(jnp.bfloat16)
    own_lists.wait()
    all_counts.wait()
    most, qblocks = listed.shape[1], listed.shape[2]
    block_of = lax.broadcasted_iota(jnp.int32, (flags, qblocks), 0)

    def mask(j, carry):
        used = jnp.broadcast_to(counted[pl.ds(place * heads + j, 1), :], (most, qblocks))
        at = lax.broadcasted_iota(jnp.int32, (most, qblocks), 0)
        entries = jnp.where(at < used, listed[j], -1)
        member = jnp.full((flags, qblocks), NEGATIVE, jnp.float32)
        for i in range(most):
            member = jnp.where(entries[i : i + 1] == block_of, 0.0, member)
        bias[j] = member.T
        return carry

    lax.fori_loop(0, heads, mask, 0)

    @pl.when(is_mid)
    def _():
        mid_outer(0)
        mid_outer(1)
        mid_own(2)

    @pl.when(is_edge)
    def _():
        edge_own(2)
        edge_queries(shared[0])
        edge_own(3)

    middle = [(0, 0), (1, 0)]
    for j in range(2, heads):
        middle += [(j, 1), (j, 0)] if j in shared else [(j, 0)]
    groups = len(middle)

    def mid_before(g):
        j, is_far = middle[g]
        first = g == 0 or middle[g - 1][0] != j
        if g == 1:
            mid_outer(2)
            mid_own(3)
        if g == 2:
            for i in range(4, heads - 1):
                mid_own(i)
        if g > 2 and middle[g - 1][0] + 1 < heads and not is_far:
            i = middle[g - 1][0] + 1
            if not first:
                mid_outer(i)
            elif i + 1 < heads:
                mid_outer(i + 1)
                if i + 2 < heads:
                    mid_own(i + 2)
        if first:
            mid_inner(j)
        if is_far:
            mid_far(j)
        else:
            queries(j)

    def edge_before(g):
        if g == 1:
            edge_own(4)
            edge_queries(shared[1])
        if g == 2:
            for j in range(5, heads):
                edge_own(j)
            for j in shared[2:]:
                edge_queries(j)
        edge_ready(kept[g])

    def group(g, carry):
        for k in range(groups):
            pl.when(jnp.logical_and(is_mid, g == k))(functools.partial(mid_before, k))
        for k in range(near):
            pl.when(jnp.logical_and(is_edge, g == k))(functools.partial(edge_before, k))
        is_far = (1 - edge) * pick(g, [f for _, f in middle])
        j = edge * pick(g, kept + [0] * (groups - near)) + (1 - edge) * pick(g, [j for j, _ in middle])
        at = (1 - edge) * pick(g, [shared.index(j) if f else 0 for j, f in middle])
        slot = j + is_far * (heads + at - j)
        plane = z + is_far * (partner - z)
        cols = columns(place, j)
        source = [mix(place, (t + 1) % side, side) for t in range(side)]

        def attend(ahead, now):
            if ahead is not None:
                flag = [
                    jnp.broadcast_to(
                        bias[j, pl.ds((plane * side + source[ahead]) * spans + b, 1), :], (BLOCK, flags)
                    ).astype(jnp.bfloat16)
                    for b in range(spans)
                ]
                query = jnp.concatenate(
                    [qbuf[slot, source[ahead]], jnp.concatenate(flag, axis=0)], axis=1
                )
                largest = None
            if now is not None:
                top = tops[now % 2]
                mixed = None
            for p in range(planes):
                span = slice(p * plane_keys, (p + 1) * plane_keys)
                if ahead is not None:
                    key = jnp.concatenate([kbuf[j, p], hot[span]], axis=1)
                    part = lax.dot_general(
                        query, key, (((1,), (1,)), ((), ())), preferred_element_type=jnp.float32
                    )
                    scores[ahead % 2, :, span] = part
                    for i in range(0, plane_keys, HEAD_DIM):
                        piece = part[:, i : i + HEAD_DIM]
                        largest = piece if largest is None else jnp.maximum(largest, piece)
                if now is not None:
                    weights = jnp.concatenate(
                        [
                            jnp.exp2((scores[now % 2, :, pl.ds(p * plane_keys + i, HEAD_DIM)] - top) * scaling)
                            .astype(jnp.bfloat16)
                            for i in range(0, plane_keys, HEAD_DIM)
                        ],
                        axis=1,
                    )
                    value = jnp.concatenate(
                        [vbuf[j, p], jnp.ones((plane_keys, HEAD_DIM), jnp.bfloat16)], axis=1
                    )
                    part = jnp.dot(weights, value, preferred_element_type=jnp.float32)
                    mixed = part if mixed is None else mixed + part
            if ahead is not None:
                tops[ahead % 2] = jnp.broadcast_to(
                    jnp.max(largest, axis=1, keepdims=True), (rows, HEAD_DIM)
                )
            if now is not None:
                obuf[slot, source[now]] = (mixed[:, :HEAD_DIM] / mixed[:, HEAD_DIM:]).astype(jnp.bfloat16)

        def send(t):
            remote(
                obuf.at[slot, source[t]], o_any.at[:, cols],
                o_send.at[is_far], o_recv.at[is_far], plane, source[t],
            )

        attend(0, None)
        for t in range(side - 1):
            attend(t + 1, t)
            send(t)
        attend(None, side - 1)
        pl.when(is_far == 1)(lambda: send(side - 1))

        @pl.when(is_far == 0)
        def _():
            pltpu.make_async_copy(obuf.at[slot, place], o_any.at[:, cols], o_home).start()

        return carry

    lax.fori_loop(0, edge * near + (1 - edge) * groups, group, 0)

    others = pl.ds(0, side - 1)
    drain(kbuf.at[:, 0, pl.ds(0, (side - 1) * key_rows)], flat_send.at[0])
    drain(vbuf.at[:, 0, pl.ds(0, (side - 1) * key_rows)], flat_send.at[1])
    drain(qbuf.at[pl.ds(0, heads), others], flat_send.at[2])

    @pl.when(is_mid)
    def _():
        for i, buf in enumerate((kbuf, vbuf)):
            drain(buf.at[:, pl.ds(0, 2)], line_send.at[0, i])
            drain(buf.at[pl.ds(0, near), pl.ds(0, 3)], line_send.at[1, i])
        drain(obuf.at[pl.ds(0, heads), 0], o_home)
        drain(obuf.at[pl.ds(0, heads), others], o_send.at[0])
        drain(obuf.at[pl.ds(0, far)], o_send.at[1])
        drain(obuf.at[pl.ds(0, heads), others], o_recv.at[0])

    @pl.when(is_edge)
    def _():
        for i, buf in enumerate((kbuf, vbuf)):
            drain(buf.at[:, 0], line_send.at[1, i])
        drain(qbuf.at[pl.ds(0, far)], far_send)
        drain(obuf.at[pl.ds(0, near), 0], o_home)
        drain(obuf.at[pl.ds(0, near), others], o_send.at[0])
        drain(obuf.at[pl.ds(0, near), others], o_recv.at[0])
        drain(obuf.at[pl.ds(0, far)], o_recv.at[1])


def flagged(lists, counts, key_blocks):
    listed = lists.shape[2]
    usable = jnp.arange(listed, dtype=jnp.int32) < counts[:, :, None]
    chosen = jnp.where(usable, lists, -1)
    flags = -(-key_blocks // HEAD_DIM) * HEAD_DIM
    blocks = jnp.arange(flags, dtype=jnp.int32)
    member = jnp.any(chosen[:, :, :, None] == blocks, axis=2)
    return jnp.where(member, 0.0, NEGATIVE).astype(jnp.float32)


LINE = 4
CORES = 2


def shared_heads(heads):
    return [2] + list(range(4, heads))


def fits_line(blk_n, uly_n, heads_all, rows):
    side = blk_n // LINE * uly_n
    return (
        blk_n == LINE * 2 * CORES and uly_n == 2
        and heads_all % side == 0 and 5 <= heads_all // side <= 6
        and rows % BLOCK == 0
    )


def along_line(blk_n, uly_n, queries, keys, values, block_lists, block_counts):
    heads_all, qblocks_all, listed = block_lists.shape
    devices, planes = blk_n * uly_n, LINE
    per_blk = blk_n // planes
    side = per_blk * uly_n
    heads = heads_all // side
    slots = heads + len(shared_heads(heads))
    rows, key_rows = queries.shape[0], keys.shape[0]
    keys_all = key_rows * devices
    flags = -(-(keys_all // BLOCK) // HEAD_DIM) * HEAD_DIM

    any_spec = pl.BlockSpec(memory_space=pl.ANY)
    dma = pltpu.SemaphoreType.DMA
    plane_keys = side * key_rows
    return pl.pallas_call(
        functools.partial(line_kernel, planes, per_blk, uly_n),
        out_shape=jax.ShapeDtypeStruct(queries.shape, queries.dtype),
        in_specs=[any_spec] * 5,
        out_specs=any_spec,
        scratch_shapes=[
            pltpu.VMEM((slots, side, rows, HEAD_DIM), jnp.bfloat16),
            pltpu.VMEM((heads, planes, plane_keys, HEAD_DIM), jnp.bfloat16),
            pltpu.VMEM((heads, planes, plane_keys, HEAD_DIM), jnp.bfloat16),
            pltpu.VMEM((slots, side, rows, HEAD_DIM), jnp.bfloat16),
            pltpu.VMEM((keys_all, flags), jnp.bfloat16),
            pltpu.VMEM((heads, qblocks_all, flags), jnp.float32),
            pltpu.VMEM((heads, listed, qblocks_all), jnp.int32),
            pltpu.VMEM((heads_all, qblocks_all), jnp.int32),
            pltpu.VMEM((2, rows, keys_all), jnp.float32),
            pltpu.VMEM((2, rows, HEAD_DIM), jnp.float32),
            dma((heads,)), dma((heads,)), dma((heads,)),
            dma((heads, planes)), dma((heads, planes)), dma((slots - heads,)),
            dma((3,)), dma((2, 2)), dma, dma((2,)), dma((2,)), dma, dma((2,)),
        ],
        compiler_params=pltpu.CompilerParams(
            collective_id=1, has_side_effects=True, vmem_limit_bytes=60 * 1024 * 1024
        ),
    )(queries, keys, values, jnp.swapaxes(block_lists, 1, 2), block_counts)


def local(blk_n, uly_n, queries, keys, values, block_lists, block_counts):
    heads_all, qblocks_all, listed = block_lists.shape
    if fits_line(blk_n, uly_n, heads_all, queries.shape[0]):
        return along_line(blk_n, uly_n, queries, keys, values, block_lists, block_counts)
    share = math.gcd(blk_n, heads_all // uly_n)
    group = share * uly_n
    heads = heads_all // group
    groups = blk_n // share
    qblocks = qblocks_all // groups
    devices = blk_n * uly_n
    rows, key_rows = queries.shape[0], keys.shape[0]
    width = heads * HEAD_DIM
    keys_all = key_rows * devices

    me = lax.axis_index("blk") * uly_n + lax.axis_index("uly")
    place = lax.rem(me, group)
    lists = lax.dynamic_slice(
        block_lists, (place * heads, (me // group) * qblocks, 0), (heads, qblocks, listed)
    )
    counts = lax.dynamic_slice(
        block_counts, (place * heads, (me // group) * qblocks), (heads, qblocks)
    )
    bias = flagged(lists, counts, keys_all // BLOCK)
    flags = bias.shape[2]

    any_spec = pl.BlockSpec(memory_space=pl.ANY)
    dma = pltpu.SemaphoreType.DMA
    return pl.pallas_call(
        functools.partial(attend_kernel, blk_n, uly_n, group),
        out_shape=jax.ShapeDtypeStruct(queries.shape, queries.dtype),
        in_specs=[any_spec, any_spec, any_spec, pl.BlockSpec(memory_space=pltpu.VMEM)],
        out_specs=any_spec,
        scratch_shapes=[
            pltpu.VMEM((group, rows, width), jnp.bfloat16),
            pltpu.VMEM((devices, key_rows, width), jnp.bfloat16),
            pltpu.VMEM((devices, key_rows, width), jnp.bfloat16),
            pltpu.VMEM((group, rows, width), jnp.bfloat16),
            pltpu.VMEM((keys_all, flags), jnp.bfloat16),
            dma((2,)), dma, dma, dma, dma((group,)), dma, dma, dma((4,)),
        ],
        compiler_params=pltpu.CompilerParams(
            collective_id=0, has_side_effects=True, vmem_limit_bytes=60 * 1024 * 1024
        ),
    )(queries, keys, values, bias)


def solution(mesh):
    return jax.shard_map(
        functools.partial(local, mesh.shape["blk"], mesh.shape["uly"]),
        mesh=mesh,
        in_specs=(
            P(("blk", "uly"), None),
            P(("blk", "uly"), None),
            P(("blk", "uly"), None),
            P(),
            P(),
        ),
        out_specs=P(("blk", "uly"), None),
        check_vma=False,
    )
```

```python
import functools
import math

import jax
import jax.numpy as jnp
from jax import lax
from jax.experimental import pallas as pl
from jax.experimental.pallas import tpu as pltpu
from jax.sharding import PartitionSpec as P

HEAD_DIM = 128
BLOCK = 128
NEGATIVE = -1e30
MESH = pl.DeviceIdType.MESH


def mix(a, b, n):
    if n & (n - 1):
        return lax.rem(n + b - a, n)
    out, bit = 0, 1
    while bit < n:
        out = out + lax.rem(a // bit + b // bit, 2) * bit
        bit *= 2
    return out


def attend_kernel(
    blk_n, uly_n, group, q_any, k_any, v_any, bias_ref, o_any,
    qbuf, kbuf, vbuf, obuf, hot,
    kv_send, k_recv, v_recv, q_send, q_recv, o_send, o_recv, local_sem,
):
    devices = blk_n * uly_n
    me = lax.axis_index("blk") * uly_n + lax.axis_index("uly")
    first = (me // group) * group
    place = me - first
    rows = q_any.shape[0]
    width = qbuf.shape[2]
    heads = width // HEAD_DIM
    keys_all = kbuf.shape[0] * kbuf.shape[1]
    flags = bias_ref.shape[2]
    scaling = math.log2(math.e) / math.sqrt(HEAD_DIM)

    def coords(device):
        return (device // uly_n, lax.rem(device, uly_n))

    def columns(position):
        return pl.ds(pl.multiple_of(position * width, HEAD_DIM), width)

    own = (
        pltpu.make_async_copy(k_any.at[:, columns(place)], kbuf.at[me], local_sem.at[0]),
        pltpu.make_async_copy(v_any.at[:, columns(place)], vbuf.at[me], local_sem.at[1]),
        pltpu.make_async_copy(q_any.at[:, columns(place)], qbuf.at[place], local_sem.at[2]),
    )
    for copy in own:
        copy.start()

    barrier = pltpu.get_barrier_semaphore()

    def greet(step, carry):
        other = lax.rem(me + step, devices)
        pl.semaphore_signal(barrier, inc=1, device_id=coords(other), device_id_type=MESH)
        return carry

    lax.fori_loop(1, devices, greet, 0)
    pl.semaphore_wait(barrier, devices - 1)

    def send_kv(step, carry):
        other = mix(me, step, devices)
        cols = columns(lax.rem(other, group))
        pltpu.make_async_remote_copy(
            src_ref=k_any.at[:, cols], dst_ref=kbuf.at[me],
            send_sem=kv_send.at[0], recv_sem=k_recv,
            device_id=coords(other), device_id_type=MESH,
        ).start()
        pltpu.make_async_remote_copy(
            src_ref=v_any.at[:, cols], dst_ref=vbuf.at[me],
            send_sem=kv_send.at[1], recv_sem=v_recv,
            device_id=coords(other), device_id_type=MESH,
        ).start()
        return carry

    lax.fori_loop(1, devices, send_kv, 0)

    def send_q(step, carry):
        there = mix(place, step, group)
        pltpu.make_async_remote_copy(
            src_ref=q_any.at[:, columns(there)], dst_ref=qbuf.at[place],
            send_sem=q_send, recv_sem=q_recv.at[place],
            device_id=coords(first + there), device_id_type=MESH,
        ).start()
        return carry

    lax.fori_loop(1, group, send_q, 0)

    key_block = lax.broadcasted_iota(jnp.int32, hot.shape, 0) // BLOCK
    lane = lax.broadcasted_iota(jnp.int32, hot.shape, 1)
    hot[...] = jnp.where(key_block == lane, 1.0, 0.0).astype(jnp.bfloat16)

    for copy in own:
        copy.wait()
    rest = pl.ds(0, devices - 1)
    pltpu.make_async_copy(kbuf.at[rest], kbuf.at[rest], k_recv).wait()
    pltpu.make_async_copy(vbuf.at[rest], vbuf.at[rest], v_recv).wait()

    def attend(source):
        for head in range(heads):
            cols = slice(head * HEAD_DIM, (head + 1) * HEAD_DIM)
            spans = max(rows // BLOCK, 1)
            flag = [
                jnp.broadcast_to(
                    bias_ref[head, pl.ds((source * rows) // BLOCK + b, 1), :],
                    (rows // spans, flags),
                ).astype(jnp.bfloat16)
                for b in range(spans)
            ]
            query = jnp.concatenate([qbuf[source, :, cols], jnp.concatenate(flag, axis=0)], axis=1)
            key = jnp.concatenate(
                [kbuf[:, :, cols].reshape(keys_all, HEAD_DIM), hot[...]], axis=1
            )
            value = vbuf[:, :, cols].reshape(keys_all, HEAD_DIM)
            scores = lax.dot_general(
                query, key, (((1,), (1,)), ((), ())), preferred_element_type=jnp.float32
            )
            top = jnp.max(scores, axis=1, keepdims=True)
            weights = jnp.exp2((scores - top) * scaling)
            total = jnp.sum(weights, axis=1, keepdims=True)
            mixed = jnp.dot(
                weights.astype(jnp.bfloat16), value, preferred_element_type=jnp.float32
            )
            obuf[source, :, cols] = (mixed / total).astype(jnp.bfloat16)

    attend(place)
    home = pltpu.make_async_copy(
        obuf.at[place], o_any.at[:, columns(place)], local_sem.at[3]
    )
    home.start()

    def visit(step, carry):
        source = mix(place, step, group)
        pltpu.make_async_copy(qbuf.at[source], qbuf.at[source], q_recv.at[source]).wait()
        attend(source)
        pltpu.make_async_remote_copy(
            src_ref=obuf.at[source], dst_ref=o_any.at[:, columns(place)],
            send_sem=o_send, recv_sem=o_recv,
            device_id=coords(first + source), device_id_type=MESH,
        ).start()
        return carry

    lax.fori_loop(1, group, visit, 0)
    home.wait()
    pltpu.make_async_copy(kbuf.at[rest], kbuf.at[rest], kv_send.at[0]).wait()
    pltpu.make_async_copy(vbuf.at[rest], vbuf.at[rest], kv_send.at[1]).wait()
    peers = pl.ds(0, group - 1)
    pltpu.make_async_copy(qbuf.at[peers], qbuf.at[peers], q_send).wait()
    pltpu.make_async_copy(obuf.at[peers], obuf.at[peers], o_send).wait()
    pltpu.make_async_copy(obuf.at[peers], obuf.at[peers], o_recv).wait()


def pick(index, entries):
    value, n = entries[0], len(entries)
    for at in range(1, n):
        value = value + (entries[at] - entries[at - 1]) * ((index - at + n) // n)
    return value


def line_kernel(
    planes, per_blk, uly_n, q_any, k_any, v_any, lists_any, counts_any, o_any,
    qbuf, kbuf, vbuf, obuf, hot, bias, listed, counted, scores, tops,
    k_in, v_in, q_in, k_line, v_line, far_in,
    flat_send, line_send, far_send, o_send, o_recv, o_home, list_in,
):
    side = per_blk * uly_n
    blk, uly = lax.axis_index("blk"), lax.axis_index("uly")
    z = blk // per_blk
    place = lax.rem(blk, per_blk) * uly_n + uly
    partner = z + 1 - 2 * lax.rem(z, 2)
    across = planes - 1 - z
    beyond = across + 1 - 2 * lax.rem(across, 2)
    edge = (z + 1) // planes + (planes - z) // planes
    is_edge, is_mid = edge == 1, edge == 0
    rows, key_rows = q_any.shape[0], k_any.shape[0]
    heads = kbuf.shape[0]
    shared = shared_heads(heads)
    kept = [j for j in range(heads) if j not in shared]
    far, near = len(shared), len(kept)
    plane_keys = kbuf.shape[2]
    keys_all = planes * plane_keys
    flags = bias.shape[2]
    scaling = math.log2(math.e) / math.sqrt(HEAD_DIM)
    spans = rows // BLOCK

    def coords(plane, position):
        return (plane * per_blk + position // uly_n, lax.rem(position, uly_n))

    def columns(position, j):
        return pl.ds(pl.multiple_of((position * heads + j) * HEAD_DIM, HEAD_DIM), HEAD_DIM)

    def remote(src, dst, send, recv, plane, position):
        pltpu.make_async_remote_copy(
            src_ref=src, dst_ref=dst, send_sem=send, recv_sem=recv,
            device_id=coords(plane, position), device_id_type=MESH,
        ).start()

    def drain(ref, sem):
        pltpu.make_async_copy(ref, ref, sem).wait()

    mine = pl.ds(pl.multiple_of(place * key_rows, key_rows), key_rows)

    barrier = pltpu.get_barrier_semaphore()

    def greet(plane, first):
        def signal(step, carry):
            other = coords(plane, mix(place, step, side))
            pl.semaphore_signal(barrier, inc=1, device_id=other, device_id_type=MESH)
            return carry

        lax.fori_loop(first, side, signal, 0)

    greet(z, 1)
    greet(partner, 0)

    @pl.when(is_mid)
    def _():
        pl.semaphore_signal(barrier, inc=1, device_id=coords(across, place), device_id_type=MESH)

    own_lists = pltpu.make_async_copy(lists_any.at[pl.ds(place * heads, heads)], listed, list_in.at[0])
    all_counts = pltpu.make_async_copy(counts_any, counted, list_in.at[1])
    own_lists.start()
    all_counts.start()
    for j in range(heads):
        cols = columns(place, j)
        pltpu.make_async_copy(k_any.at[:, cols], kbuf.at[j, z, mine], k_in.at[j]).start()
        pltpu.make_async_copy(v_any.at[:, cols], vbuf.at[j, z, mine], v_in.at[j]).start()
        pltpu.make_async_copy(q_any.at[:, cols], qbuf.at[j, place], q_in.at[j]).start()

    pl.semaphore_wait(barrier, 2 * side - edge)

    def send_kv(j):
        def body(step, carry):
            other = mix(place, step, side)
            cols = columns(other, j)
            remote(k_any.at[:, cols], kbuf.at[j, z, mine], flat_send.at[0], k_in.at[j], z, other)
            remote(v_any.at[:, cols], vbuf.at[j, z, mine], flat_send.at[1], v_in.at[j], z, other)
            return carry

        lax.fori_loop(1, side, body, 0)

    def send_q(j):
        def body(step, carry):
            other = mix(place, step, side)
            cols = columns(other, j)
            remote(q_any.at[:, cols], qbuf.at[j, place], flat_send.at[2], q_in.at[j], z, other)
            return carry

        lax.fori_loop(1, side, body, 0)

    def hand(j, block, plane, way):
        for buf, sem, arrived in ((kbuf, line_send.at[way, 0], k_line), (vbuf, line_send.at[way, 1], v_line)):
            remote(buf.at[j, block], buf.at[j, block], sem, arrived.at[j, block], plane, place)

    def lines(way):
        return ((k_any, kbuf, line_send.at[way, 0], k_line), (v_any, vbuf, line_send.at[way, 1], v_line))

    def hand_mine(j, plane, way):
        for source, buf, sem, arrived in lines(way):
            remote(
                source.at[:, columns(place, j)], buf.at[j, z, mine], sem, arrived.at[j, z], plane, place
            )

    def hand_rest(j, plane, way):
        size = side // 2
        while size:
            start = (place // size + 1 - 2 * lax.rem(place // size, 2)) * size * key_rows
            part = pl.ds(pl.multiple_of(start, key_rows), size * key_rows)
            for _, buf, sem, arrived in lines(way):
                remote(buf.at[j, z, part], buf.at[j, z, part], sem, arrived.at[j, z], plane, place)
            size //= 2

    def arrive(j, block):
        drain(kbuf.at[j, block], k_line.at[j, block])
        drain(vbuf.at[j, block], v_line.at[j, block])

    def queries(j):
        drain(qbuf.at[j], q_in.at[j])

    def edge_own(j):
        drain(kbuf.at[j, z], k_in.at[j])
        drain(vbuf.at[j, z], v_in.at[j])
        hand_rest(j, partner, 1)

    def edge_queries(j):
        queries(j)
        at = shared.index(j)
        remote(qbuf.at[j], qbuf.at[heads + at], far_send, far_in.at[at], partner, place)

    def edge_ready(j):
        for block in (partner, beyond, across):
            arrive(j, block)
        queries(j)

    def mid_own(j):
        drain(kbuf.at[j, z], k_in.at[j])
        drain(vbuf.at[j, z], v_in.at[j])
        hand_rest(j, across, 0)
        if j in kept:
            hand_rest(j, partner, 1)

    def mid_outer(j):
        arrive(j, partner)
        hand(j, partner, across, 0)

    def mid_inner(j):
        for block in (across, beyond):
            arrive(j, block)
            if j in kept:
                hand(j, block, partner, 1)

    def mid_far(j):
        at = shared.index(j)
        drain(qbuf.at[heads + at], far_in.at[at])

    order = ["kv0", "kv1", "q0", "own0", "kv2", "q2", "own1"]
    for j in range(3, heads):
        order.append("kv%d" % j)
        if j == 3:
            order.append("q1")
        elif j in shared:
            order.append("q%d" % j)
    order += ["q%d" % j for j in range(heads) if "q%d" % j not in order]
    def early():
        for j in range(heads):
            pl.when(is_mid)(functools.partial(hand_mine, j, across, 0))
            if j in kept:
                hand_mine(j, partner, 1)
            else:
                pl.when(is_edge)(functools.partial(hand_mine, j, partner, 1))

    for what in order:
        if what == "kv1":
            early()
        j = int(what.lstrip("kvqown"))
        if what.startswith("kv"):
            send_kv(j)
        elif what.startswith("q"):
            send_q(j)
        else:
            pl.when(is_edge)(functools.partial(edge_own, j))
            pl.when(is_mid)(functools.partial(mid_own, j))

    key_block = lax.broadcasted_iota(jnp.int32, hot.shape, 0) // BLOCK
    lane = lax.broadcasted_iota(jnp.int32, hot.shape, 1)
    hot[...] = jnp.where(key_block == lane, 1.0, 0.0).astype(jnp.bfloat16)
    own_lists.wait()
    all_counts.wait()
    most, qblocks = listed.shape[1], listed.shape[2]
    block_of = lax.broadcasted_iota(jnp.int32, (flags, qblocks), 0)

    def mask(j, carry):
        used = jnp.broadcast_to(counted[pl.ds(place * heads + j, 1), :], (most, qblocks))
        at = lax.broadcasted_iota(jnp.int32, (most, qblocks), 0)
        entries = jnp.where(at < used, listed[j], -1)
        member = jnp.full((flags, qblocks), NEGATIVE, jnp.float32)
        for i in range(most):
            member = jnp.where(entries[i : i + 1] == block_of, 0.0, member)
        bias[j] = member.T
        return carry

    lax.fori_loop(0, heads, mask, 0)

    @pl.when(is_mid)
    def _():
        mid_outer(0)
        mid_outer(1)
        mid_own(2)

    @pl.when(is_edge)
    def _():
        edge_own(2)
        edge_queries(shared[0])
        edge_own(3)

    middle = [(0, 0), (1, 0)]
    for j in range(2, heads):
        middle += [(j, 1), (j, 0)] if j in shared else [(j, 0)]
    groups = len(middle)

    def mid_before(g):
        j, is_far = middle[g]
        first = g == 0 or middle[g - 1][0] != j
        if g == 1:
            mid_outer(2)
            mid_own(3)
        if g == 2:
            for i in range(4, heads - 1):
                mid_own(i)
        if g > 2 and middle[g - 1][0] + 1 < heads and not is_far:
            i = middle[g - 1][0] + 1
            if not first:
                mid_outer(i)
            elif i + 1 < heads:
                mid_outer(i + 1)
                if i + 2 < heads:
                    mid_own(i + 2)
        if first:
            mid_inner(j)
        if is_far:
            mid_far(j)
        else:
            queries(j)

    def edge_before(g):
        if g == 1:
            edge_own(4)
            edge_queries(shared[1])
        if g == 2:
            for j in range(5, heads):
                edge_own(j)
            for j in shared[2:]:
                edge_queries(j)
        edge_ready(kept[g])

    def group(g, carry):
        for k in range(groups):
            pl.when(jnp.logical_and(is_mid, g == k))(functools.partial(mid_before, k))
        for k in range(near):
            pl.when(jnp.logical_and(is_edge, g == k))(functools.partial(edge_before, k))
        is_far = (1 - edge) * pick(g, [f for _, f in middle])
        j = edge * pick(g, kept + [0] * (groups - near)) + (1 - edge) * pick(g, [j for j, _ in middle])
        at = (1 - edge) * pick(g, [shared.index(j) if f else 0 for j, f in middle])
        slot = j + is_far * (heads + at - j)
        plane = z + is_far * (partner - z)
        cols = columns(place, j)
        source = [mix(place, (t + 1) % side, side) for t in range(side)]

        def attend(ahead, now):
            if ahead is not None:
                flag = [
                    jnp.broadcast_to(
                        bias[j, pl.ds((plane * side + source[ahead]) * spans + b, 1), :], (BLOCK, flags)
                    ).astype(jnp.bfloat16)
                    for b in range(spans)
                ]
                query = jnp.concatenate(
                    [qbuf[slot, source[ahead]], jnp.concatenate(flag, axis=0)], axis=1
                )
                largest = None
            if now is not None:
                top = tops[now % 2]
                mixed = None
            for p in range(planes):
                span = slice(p * plane_keys, (p + 1) * plane_keys)
                if ahead is not None:
                    key = jnp.concatenate([kbuf[j, p], hot[span]], axis=1)
                    part = lax.dot_general(
                        query, key, (((1,), (1,)), ((), ())), preferred_element_type=jnp.float32
                    )
                    scores[ahead % 2, :, span] = part
                    for i in range(0, plane_keys, HEAD_DIM):
                        piece = part[:, i : i + HEAD_DIM]
                        largest = piece if largest is None else jnp.maximum(largest, piece)
                if now is not None:
                    weights = jnp.concatenate(
                        [
                            jnp.exp2((scores[now % 2, :, pl.ds(p * plane_keys + i, HEAD_DIM)] - top) * scaling)
                            .astype(jnp.bfloat16)
                            for i in range(0, plane_keys, HEAD_DIM)
                        ],
                        axis=1,
                    )
                    value = jnp.concatenate(
                        [vbuf[j, p], jnp.ones((plane_keys, HEAD_DIM), jnp.bfloat16)], axis=1
                    )
                    part = jnp.dot(weights, value, preferred_element_type=jnp.float32)
                    mixed = part if mixed is None else mixed + part
            if ahead is not None:
                tops[ahead % 2] = jnp.broadcast_to(
                    jnp.max(largest, axis=1, keepdims=True), (rows, HEAD_DIM)
                )
            if now is not None:
                obuf[slot, source[now]] = (mixed[:, :HEAD_DIM] / mixed[:, HEAD_DIM:]).astype(jnp.bfloat16)

        def send(t):
            remote(
                obuf.at[slot, source[t]], o_any.at[:, cols],
                o_send.at[is_far], o_recv.at[is_far], plane, source[t],
            )

        attend(0, None)
        for t in range(side - 1):
            attend(t + 1, t)
            send(t)
        attend(None, side - 1)
        pl.when(is_far == 1)(lambda: send(side - 1))

        @pl.when(is_far == 0)
        def _():
            pltpu.make_async_copy(obuf.at[slot, place], o_any.at[:, cols], o_home).start()

        return carry

    lax.fori_loop(0, edge * near + (1 - edge) * groups, group, 0)

    others = pl.ds(0, side - 1)
    drain(kbuf.at[:, 0, pl.ds(0, (side - 1) * key_rows)], flat_send.at[0])
    drain(vbuf.at[:, 0, pl.ds(0, (side - 1) * key_rows)], flat_send.at[1])
    drain(qbuf.at[pl.ds(0, heads), others], flat_send.at[2])

    @pl.when(is_mid)
    def _():
        for i, buf in enumerate((kbuf, vbuf)):
            drain(buf.at[:, pl.ds(0, 2)], line_send.at[0, i])
            drain(buf.at[pl.ds(0, near), pl.ds(0, 3)], line_send.at[1, i])
        drain(obuf.at[pl.ds(0, heads), 0], o_home)
        drain(obuf.at[pl.ds(0, heads), others], o_send.at[0])
        drain(obuf.at[pl.ds(0, far)], o_send.at[1])
        drain(obuf.at[pl.ds(0, heads), others], o_recv.at[0])

    @pl.when(is_edge)
    def _():
        for i, buf in enumerate((kbuf, vbuf)):
            drain(buf.at[:, 0], line_send.at[1, i])
        drain(qbuf.at[pl.ds(0, far)], far_send)
        drain(obuf.at[pl.ds(0, near), 0], o_home)
        drain(obuf.at[pl.ds(0, near), others], o_send.at[0])
        drain(obuf.at[pl.ds(0, near), others], o_recv.at[0])
        drain(obuf.at[pl.ds(0, far)], o_recv.at[1])


def flagged(lists, counts, key_blocks):
    listed = lists.shape[2]
    usable = jnp.arange(listed, dtype=jnp.int32) < counts[:, :, None]
    chosen = jnp.where(usable, lists, -1)
    flags = -(-key_blocks // HEAD_DIM) * HEAD_DIM
    blocks = jnp.arange(flags, dtype=jnp.int32)
    member = jnp.any(chosen[:, :, :, None] == blocks, axis=2)
    return jnp.where(member, 0.0, NEGATIVE).astype(jnp.float32)


LINE = 4
CORES = 2


def shared_heads(heads):
    return [2] + list(range(4, heads))


def fits_line(blk_n, uly_n, heads_all, rows):
    side = blk_n // LINE * uly_n
    return (
        blk_n == LINE * 2 * CORES and uly_n == 2
        and heads_all % side == 0 and 5 <= heads_all // side <= 6
        and rows % BLOCK == 0
    )


def along_line(blk_n, uly_n, queries, keys, values, block_lists, block_counts):
    heads_all, qblocks_all, listed = block_lists.shape
    devices, planes = blk_n * uly_n, LINE
    per_blk = blk_n // planes
    side = per_blk * uly_n
    heads = heads_all // side
    slots = heads + len(shared_heads(heads))
    rows, key_rows = queries.shape[0], keys.shape[0]
    keys_all = key_rows * devices
    flags = -(-(keys_all // BLOCK) // HEAD_DIM) * HEAD_DIM

    any_spec = pl.BlockSpec(memory_space=pl.ANY)
    dma = pltpu.SemaphoreType.DMA
    plane_keys = side * key_rows
    return pl.pallas_call(
        functools.partial(line_kernel, planes, per_blk, uly_n),
        out_shape=jax.ShapeDtypeStruct(queries.shape, queries.dtype),
        in_specs=[any_spec] * 5,
        out_specs=any_spec,
        scratch_shapes=[
            pltpu.VMEM((slots, side, rows, HEAD_DIM), jnp.bfloat16),
            pltpu.VMEM((heads, planes, plane_keys, HEAD_DIM), jnp.bfloat16),
            pltpu.VMEM((heads, planes, plane_keys, HEAD_DIM), jnp.bfloat16),
            pltpu.VMEM((slots, side, rows, HEAD_DIM), jnp.bfloat16),
            pltpu.VMEM((keys_all, flags), jnp.bfloat16),
            pltpu.VMEM((heads, qblocks_all, flags), jnp.float32),
            pltpu.VMEM((heads, listed, qblocks_all), jnp.int32),
            pltpu.VMEM((heads_all, qblocks_all), jnp.int32),
            pltpu.VMEM((2, rows, keys_all), jnp.float32),
            pltpu.VMEM((2, rows, HEAD_DIM), jnp.float32),
            dma((heads,)), dma((heads,)), dma((heads,)),
            dma((heads, planes)), dma((heads, planes)), dma((slots - heads,)),
            dma((3,)), dma((2, 2)), dma, dma((2,)), dma((2,)), dma, dma((2,)),
        ],
        compiler_params=pltpu.CompilerParams(
            collective_id=1, has_side_effects=True, vmem_limit_bytes=40 * 1024 * 1024
        ),
    )(*(pltpu.with_memory_space_constraint(a, pltpu.HBM) for a in (queries, keys, values, jnp.swapaxes(block_lists, 1, 2), block_counts)))


def local(blk_n, uly_n, queries, keys, values, block_lists, block_counts):
    heads_all, qblocks_all, listed = block_lists.shape
    if fits_line(blk_n, uly_n, heads_all, queries.shape[0]):
        return along_line(blk_n, uly_n, queries, keys, values, block_lists, block_counts)
    share = math.gcd(blk_n, heads_all // uly_n)
    group = share * uly_n
    heads = heads_all // group
    groups = blk_n // share
    qblocks = qblocks_all // groups
    devices = blk_n * uly_n
    rows, key_rows = queries.shape[0], keys.shape[0]
    width = heads * HEAD_DIM
    keys_all = key_rows * devices

    me = lax.axis_index("blk") * uly_n + lax.axis_index("uly")
    place = lax.rem(me, group)
    lists = lax.dynamic_slice(
        block_lists, (place * heads, (me // group) * qblocks, 0), (heads, qblocks, listed)
    )
    counts = lax.dynamic_slice(
        block_counts, (place * heads, (me // group) * qblocks), (heads, qblocks)
    )
    bias = flagged(lists, counts, keys_all // BLOCK)
    flags = bias.shape[2]

    any_spec = pl.BlockSpec(memory_space=pl.ANY)
    dma = pltpu.SemaphoreType.DMA
    return pl.pallas_call(
        functools.partial(attend_kernel, blk_n, uly_n, group),
        out_shape=jax.ShapeDtypeStruct(queries.shape, queries.dtype),
        in_specs=[any_spec, any_spec, any_spec, pl.BlockSpec(memory_space=pltpu.VMEM)],
        out_specs=any_spec,
        scratch_shapes=[
            pltpu.VMEM((group, rows, width), jnp.bfloat16),
            pltpu.VMEM((devices, key_rows, width), jnp.bfloat16),
            pltpu.VMEM((devices, key_rows, width), jnp.bfloat16),
            pltpu.VMEM((group, rows, width), jnp.bfloat16),
            pltpu.VMEM((keys_all, flags), jnp.bfloat16),
            dma((2,)), dma, dma, dma, dma((group,)), dma, dma, dma((4,)),
        ],
        compiler_params=pltpu.CompilerParams(
            collective_id=0, has_side_effects=True, vmem_limit_bytes=60 * 1024 * 1024
        ),
    )(queries, keys, values, bias)


def solution(mesh):
    return jax.shard_map(
        functools.partial(local, mesh.shape["blk"], mesh.shape["uly"]),
        mesh=mesh,
        in_specs=(
            P(("blk", "uly"), None),
            P(("blk", "uly"), None),
            P(("blk", "uly"), None),
            P(),
            P(),
        ),
        out_specs=P(("blk", "uly"), None),
        check_vma=False,
    )
```

```python
import functools
import math

import jax
import jax.numpy as jnp
from jax import lax
from jax.experimental import pallas as pl
from jax.experimental.pallas import tpu as pltpu
from jax.sharding import PartitionSpec as P

HEAD_DIM = 128
BLOCK = 128
NEGATIVE = -1e30
MESH = pl.DeviceIdType.MESH


def mix(a, b, n):
    if n & (n - 1):
        return lax.rem(n + b - a, n)
    out, bit = 0, 1
    while bit < n:
        out = out + lax.rem(a // bit + b // bit, 2) * bit
        bit *= 2
    return out


def attend_kernel(
    blk_n, uly_n, group, q_any, k_any, v_any, bias_ref, o_any,
    qbuf, kbuf, vbuf, obuf, hot,
    kv_send, k_recv, v_recv, q_send, q_recv, o_send, o_recv, local_sem,
):
    devices = blk_n * uly_n
    me = lax.axis_index("blk") * uly_n + lax.axis_index("uly")
    first = (me // group) * group
    place = me - first
    rows = q_any.shape[0]
    width = qbuf.shape[2]
    heads = width // HEAD_DIM
    keys_all = kbuf.shape[0] * kbuf.shape[1]
    flags = bias_ref.shape[2]
    scaling = math.log2(math.e) / math.sqrt(HEAD_DIM)

    def coords(device):
        return (device // uly_n, lax.rem(device, uly_n))

    def columns(position):
        return pl.ds(pl.multiple_of(position * width, HEAD_DIM), width)

    own = (
        pltpu.make_async_copy(k_any.at[:, columns(place)], kbuf.at[me], local_sem.at[0]),
        pltpu.make_async_copy(v_any.at[:, columns(place)], vbuf.at[me], local_sem.at[1]),
        pltpu.make_async_copy(q_any.at[:, columns(place)], qbuf.at[place], local_sem.at[2]),
    )
    for copy in own:
        copy.start()

    barrier = pltpu.get_barrier_semaphore()

    def greet(step, carry):
        other = lax.rem(me + step, devices)
        pl.semaphore_signal(barrier, inc=1, device_id=coords(other), device_id_type=MESH)
        return carry

    lax.fori_loop(1, devices, greet, 0)
    pl.semaphore_wait(barrier, devices - 1)

    def send_kv(step, carry):
        other = mix(me, step, devices)
        cols = columns(lax.rem(other, group))
        pltpu.make_async_remote_copy(
            src_ref=k_any.at[:, cols], dst_ref=kbuf.at[me],
            send_sem=kv_send.at[0], recv_sem=k_recv,
            device_id=coords(other), device_id_type=MESH,
        ).start()
        pltpu.make_async_remote_copy(
            src_ref=v_any.at[:, cols], dst_ref=vbuf.at[me],
            send_sem=kv_send.at[1], recv_sem=v_recv,
            device_id=coords(other), device_id_type=MESH,
        ).start()
        return carry

    lax.fori_loop(1, devices, send_kv, 0)

    def send_q(step, carry):
        there = mix(place, step, group)
        pltpu.make_async_remote_copy(
            src_ref=q_any.at[:, columns(there)], dst_ref=qbuf.at[place],
            send_sem=q_send, recv_sem=q_recv.at[place],
            device_id=coords(first + there), device_id_type=MESH,
        ).start()
        return carry

    lax.fori_loop(1, group, send_q, 0)

    key_block = lax.broadcasted_iota(jnp.int32, hot.shape, 0) // BLOCK
    lane = lax.broadcasted_iota(jnp.int32, hot.shape, 1)
    hot[...] = jnp.where(key_block == lane, 1.0, 0.0).astype(jnp.bfloat16)

    for copy in own:
        copy.wait()
    rest = pl.ds(0, devices - 1)
    pltpu.make_async_copy(kbuf.at[rest], kbuf.at[rest], k_recv).wait()
    pltpu.make_async_copy(vbuf.at[rest], vbuf.at[rest], v_recv).wait()

    def attend(source):
        for head in range(heads):
            cols = slice(head * HEAD_DIM, (head + 1) * HEAD_DIM)
            spans = max(rows // BLOCK, 1)
            flag = [
                jnp.broadcast_to(
                    bias_ref[head, pl.ds((source * rows) // BLOCK + b, 1), :],
                    (rows // spans, flags),
                ).astype(jnp.bfloat16)
                for b in range(spans)
            ]
            query = jnp.concatenate([qbuf[source, :, cols], jnp.concatenate(flag, axis=0)], axis=1)
            key = jnp.concatenate(
                [kbuf[:, :, cols].reshape(keys_all, HEAD_DIM), hot[...]], axis=1
            )
            value = vbuf[:, :, cols].reshape(keys_all, HEAD_DIM)
            scores = lax.dot_general(
                query, key, (((1,), (1,)), ((), ())), preferred_element_type=jnp.float32
            )
            top = jnp.max(scores, axis=1, keepdims=True)
            weights = jnp.exp2((scores - top) * scaling)
            total = jnp.sum(weights, axis=1, keepdims=True)
            mixed = jnp.dot(
                weights.astype(jnp.bfloat16), value, preferred_element_type=jnp.float32
            )
            obuf[source, :, cols] = (mixed / total).astype(jnp.bfloat16)

    attend(place)
    home = pltpu.make_async_copy(
        obuf.at[place], o_any.at[:, columns(place)], local_sem.at[3]
    )
    home.start()

    def visit(step, carry):
        source = mix(place, step, group)
        pltpu.make_async_copy(qbuf.at[source], qbuf.at[source], q_recv.at[source]).wait()
        attend(source)
        pltpu.make_async_remote_copy(
            src_ref=obuf.at[source], dst_ref=o_any.at[:, columns(place)],
            send_sem=o_send, recv_sem=o_recv,
            device_id=coords(first + source), device_id_type=MESH,
        ).start()
        return carry

    lax.fori_loop(1, group, visit, 0)
    home.wait()
    pltpu.make_async_copy(kbuf.at[rest], kbuf.at[rest], kv_send.at[0]).wait()
    pltpu.make_async_copy(vbuf.at[rest], vbuf.at[rest], kv_send.at[1]).wait()
    peers = pl.ds(0, group - 1)
    pltpu.make_async_copy(qbuf.at[peers], qbuf.at[peers], q_send).wait()
    pltpu.make_async_copy(obuf.at[peers], obuf.at[peers], o_send).wait()
    pltpu.make_async_copy(obuf.at[peers], obuf.at[peers], o_recv).wait()


def pick(index, entries):
    value, n = entries[0], len(entries)
    for at in range(1, n):
        value = value + (entries[at] - entries[at - 1]) * ((index - at + n) // n)
    return value


def line_kernel(
    planes, per_blk, uly_n, q_any, k_any, v_any, lists_any, counts_any, o_any,
    qbuf, kbuf, vbuf, obuf, hot, bias, listed, counted, scores, tops,
    k_in, v_in, q_in, k_line, v_line, far_in,
    flat_send, line_send, far_send, o_send, o_recv, o_home, list_in,
):
    side = per_blk * uly_n
    blk, uly = lax.axis_index("blk"), lax.axis_index("uly")
    z = blk // per_blk
    place = lax.rem(blk, per_blk) * uly_n + uly
    partner = z + 1 - 2 * lax.rem(z, 2)
    across = planes - 1 - z
    beyond = across + 1 - 2 * lax.rem(across, 2)
    edge = (z + 1) // planes + (planes - z) // planes
    is_edge, is_mid = edge == 1, edge == 0
    rows, key_rows = q_any.shape[0], k_any.shape[0]
    heads = kbuf.shape[0]
    shared = shared_heads(heads)
    kept = [j for j in range(heads) if j not in shared]
    far, near = len(shared), len(kept)
    plane_keys = kbuf.shape[2]
    keys_all = planes * plane_keys
    flags = bias.shape[2]
    scaling = math.log2(math.e) / math.sqrt(HEAD_DIM)
    spans = rows // BLOCK

    def coords(plane, position):
        return (plane * per_blk + position // uly_n, lax.rem(position, uly_n))

    def columns(position, j):
        return pl.ds(pl.multiple_of((position * heads + j) * HEAD_DIM, HEAD_DIM), HEAD_DIM)

    def remote(src, dst, send, recv, plane, position):
        pltpu.make_async_remote_copy(
            src_ref=src, dst_ref=dst, send_sem=send, recv_sem=recv,
            device_id=coords(plane, position), device_id_type=MESH,
        ).start()

    def drain(ref, sem):
        pltpu.make_async_copy(ref, ref, sem).wait()

    mine = pl.ds(pl.multiple_of(place * key_rows, key_rows), key_rows)

    barrier = pltpu.get_barrier_semaphore()

    def greet(plane, first):
        def signal(step, carry):
            other = coords(plane, mix(place, step, side))
            pl.semaphore_signal(barrier, inc=1, device_id=other, device_id_type=MESH)
            return carry

        lax.fori_loop(first, side, signal, 0)

    greet(z, 1)
    greet(partner, 0)

    @pl.when(is_mid)
    def _():
        pl.semaphore_signal(barrier, inc=1, device_id=coords(across, place), device_id_type=MESH)

    own_lists = pltpu.make_async_copy(lists_any.at[pl.ds(place * heads, heads)], listed, list_in.at[0])
    all_counts = pltpu.make_async_copy(counts_any, counted, list_in.at[1])
    own_lists.start()
    all_counts.start()
    for j in range(heads):
        cols = columns(place, j)
        pltpu.make_async_copy(k_any.at[:, cols], kbuf.at[j, z, mine], k_in.at[j]).start()
        pltpu.make_async_copy(v_any.at[:, cols], vbuf.at[j, z, mine], v_in.at[j]).start()
        pltpu.make_async_copy(q_any.at[:, cols], qbuf.at[j, place], q_in.at[j]).start()

    pl.semaphore_wait(barrier, 2 * side - edge)

    def send_kv(j):
        def body(step, carry):
            other = mix(place, step, side)
            cols = columns(other, j)
            remote(k_any.at[:, cols], kbuf.at[j, z, mine], flat_send.at[0], k_in.at[j], z, other)
            remote(v_any.at[:, cols], vbuf.at[j, z, mine], flat_send.at[1], v_in.at[j], z, other)
            return carry

        lax.fori_loop(1, side, body, 0)

    def send_q(j):
        def body(step, carry):
            other = mix(place, step, side)
            cols = columns(other, j)
            remote(q_any.at[:, cols], qbuf.at[j, place], flat_send.at[2], q_in.at[j], z, other)
            return carry

        lax.fori_loop(1, side, body, 0)

    def hand(j, block, plane, way):
        for buf, sem, arrived in ((kbuf, line_send.at[way, 0], k_line), (vbuf, line_send.at[way, 1], v_line)):
            remote(buf.at[j, block], buf.at[j, block], sem, arrived.at[j, block], plane, place)

    def lines(way):
        return ((k_any, kbuf, line_send.at[way, 0], k_line), (v_any, vbuf, line_send.at[way, 1], v_line))

    def hand_mine(j, plane, way):
        for source, buf, sem, arrived in lines(way):
            remote(
                source.at[:, columns(place, j)], buf.at[j, z, mine], sem, arrived.at[j, z], plane, place
            )

    def hand_rest(j, plane, way):
        size = side // 2
        while size:
            start = (place // size + 1 - 2 * lax.rem(place // size, 2)) * size * key_rows
            part = pl.ds(pl.multiple_of(start, key_rows), size * key_rows)
            for _, buf, sem, arrived in lines(way):
                remote(buf.at[j, z, part], buf.at[j, z, part], sem, arrived.at[j, z], plane, place)
            size //= 2

    def arrive(j, block):
        drain(kbuf.at[j, block], k_line.at[j, block])
        drain(vbuf.at[j, block], v_line.at[j, block])

    def queries(j):
        drain(qbuf.at[j], q_in.at[j])

    def edge_own(j):
        drain(kbuf.at[j, z], k_in.at[j])
        drain(vbuf.at[j, z], v_in.at[j])
        hand_rest(j, partner, 1)

    def edge_queries(j):
        queries(j)
        at = shared.index(j)
        remote(qbuf.at[j], qbuf.at[heads + at], far_send, far_in.at[at], partner, place)

    def edge_ready(j):
        for block in (partner, beyond, across):
            arrive(j, block)
        queries(j)

    def mid_own(j):
        drain(kbuf.at[j, z], k_in.at[j])
        drain(vbuf.at[j, z], v_in.at[j])
        hand_rest(j, across, 0)
        if j in kept:
            hand_rest(j, partner, 1)

    def mid_outer(j):
        arrive(j, partner)
        hand(j, partner, across, 0)

    def mid_inner(j):
        for block in (across, beyond):
            arrive(j, block)
            if j in kept:
                hand(j, block, partner, 1)

    def mid_far(j):
        at = shared.index(j)
        drain(qbuf.at[heads + at], far_in.at[at])

    order = ["kv0", "kv1", "q0", "own0", "kv2", "q2", "own1"]
    for j in range(3, heads):
        order.append("kv%d" % j)
        if j == 3:
            order.append("q1")
        elif j in shared:
            order.append("q%d" % j)
    order += ["q%d" % j for j in range(heads) if "q%d" % j not in order]
    def early():
        for j in kept:
            hand_mine(j, partner, 1)

        @pl.when(is_edge)
        def _():
            for j in shared:
                hand_mine(j, partner, 1)

        @pl.when(is_mid)
        def _():
            for j in range(heads):
                hand_mine(j, across, 0)

    for what in order:
        if what == "kv1":
            early()
        j = int(what.lstrip("kvqown"))
        if what.startswith("kv"):
            send_kv(j)
        elif what.startswith("q"):
            send_q(j)
        else:
            pl.when(is_edge)(functools.partial(edge_own, j))
            pl.when(is_mid)(functools.partial(mid_own, j))

    key_block = lax.broadcasted_iota(jnp.int32, hot.shape, 0) // BLOCK
    lane = lax.broadcasted_iota(jnp.int32, hot.shape, 1)
    hot[...] = jnp.where(key_block == lane, 1.0, 0.0).astype(jnp.bfloat16)
    own_lists.wait()
    all_counts.wait()
    most, qblocks = listed.shape[1], listed.shape[2]
    block_of = lax.broadcasted_iota(jnp.int32, (flags, qblocks), 0)

    def mask(j, carry):
        used = jnp.broadcast_to(counted[pl.ds(place * heads + j, 1), :], (most, qblocks))
        at = lax.broadcasted_iota(jnp.int32, (most, qblocks), 0)
        entries = jnp.where(at < used, listed[j], -1)
        member = jnp.full((flags, qblocks), NEGATIVE, jnp.float32)
        for i in range(most):
            member = jnp.where(entries[i : i + 1] == block_of, 0.0, member)
        bias[j] = member.T
        return carry

    lax.fori_loop(0, heads, mask, 0)

    @pl.when(is_mid)
    def _():
        mid_outer(0)
        mid_outer(1)
        mid_own(2)

    @pl.when(is_edge)
    def _():
        edge_own(2)
        edge_queries(shared[0])
        edge_own(3)

    middle = [(0, 0), (1, 0)]
    for j in range(2, heads):
        middle += [(j, 1), (j, 0)] if j in shared else [(j, 0)]
    groups = len(middle)

    def mid_before(g):
        j, is_far = middle[g]
        first = g == 0 or middle[g - 1][0] != j
        if g == 1:
            mid_outer(2)
            mid_own(3)
        if g == 2:
            for i in range(4, heads - 1):
                mid_own(i)
        if g > 2 and middle[g - 1][0] + 1 < heads and not is_far:
            i = middle[g - 1][0] + 1
            if not first:
                mid_outer(i)
            elif i + 1 < heads:
                mid_outer(i + 1)
                if i + 2 < heads:
                    mid_own(i + 2)
        if first:
            mid_inner(j)
        if is_far:
            mid_far(j)
        else:
            queries(j)

    def edge_before(g):
        if g == 1:
            edge_own(4)
            edge_queries(shared[1])
        if g == 2:
            for j in range(5, heads):
                edge_own(j)
            for j in shared[2:]:
                edge_queries(j)
        edge_ready(kept[g])

    def group(g, carry):
        for k in range(groups):
            pl.when(jnp.logical_and(is_mid, g == k))(functools.partial(mid_before, k))
        for k in range(near):
            pl.when(jnp.logical_and(is_edge, g == k))(functools.partial(edge_before, k))
        is_far = (1 - edge) * pick(g, [f for _, f in middle])
        j = edge * pick(g, kept + [0] * (groups - near)) + (1 - edge) * pick(g, [j for j, _ in middle])
        at = (1 - edge) * pick(g, [shared.index(j) if f else 0 for j, f in middle])
        slot = j + is_far * (heads + at - j)
        plane = z + is_far * (partner - z)
        cols = columns(place, j)
        source = [mix(place, (t + 1) % side, side) for t in range(side)]

        def attend(ahead, now):
            if ahead is not None:
                flag = [
                    jnp.broadcast_to(
                        bias[j, pl.ds((plane * side + source[ahead]) * spans + b, 1), :], (BLOCK, flags)
                    ).astype(jnp.bfloat16)
                    for b in range(spans)
                ]
                query = jnp.concatenate(
                    [qbuf[slot, source[ahead]], jnp.concatenate(flag, axis=0)], axis=1
                )
                largest = None
            if now is not None:
                top = tops[now % 2]
                mixed = None
            for p in range(planes):
                span = slice(p * plane_keys, (p + 1) * plane_keys)
                if ahead is not None:
                    key = jnp.concatenate([kbuf[j, p], hot[span]], axis=1)
                    part = lax.dot_general(
                        query, key, (((1,), (1,)), ((), ())), preferred_element_type=jnp.float32
                    )
                    scores[ahead % 2, :, span] = part
                    for i in range(0, plane_keys, HEAD_DIM):
                        piece = part[:, i : i + HEAD_DIM]
                        largest = piece if largest is None else jnp.maximum(largest, piece)
                if now is not None:
                    weights = jnp.concatenate(
                        [
                            jnp.exp2((scores[now % 2, :, pl.ds(p * plane_keys + i, HEAD_DIM)] - top) * scaling)
                            .astype(jnp.bfloat16)
                            for i in range(0, plane_keys, HEAD_DIM)
                        ],
                        axis=1,
                    )
                    value = jnp.concatenate(
                        [vbuf[j, p], jnp.ones((plane_keys, HEAD_DIM), jnp.bfloat16)], axis=1
                    )
                    part = jnp.dot(weights, value, preferred_element_type=jnp.float32)
                    mixed = part if mixed is None else mixed + part
            if ahead is not None:
                tops[ahead % 2] = jnp.broadcast_to(
                    jnp.max(largest, axis=1, keepdims=True), (rows, HEAD_DIM)
                )
            if now is not None:
                obuf[slot, source[now]] = (mixed[:, :HEAD_DIM] / mixed[:, HEAD_DIM:]).astype(jnp.bfloat16)

        def send(t):
            remote(
                obuf.at[slot, source[t]], o_any.at[:, cols],
                o_send.at[is_far], o_recv.at[is_far], plane, source[t],
            )

        attend(0, None)
        for t in range(side - 1):
            attend(t + 1, t)
            send(t)
        attend(None, side - 1)
        pl.when(is_far == 1)(lambda: send(side - 1))

        @pl.when(is_far == 0)
        def _():
            pltpu.make_async_copy(obuf.at[slot, place], o_any.at[:, cols], o_home).start()

        return carry

    lax.fori_loop(0, edge * near + (1 - edge) * groups, group, 0)

    others = pl.ds(0, side - 1)
    drain(kbuf.at[:, 0, pl.ds(0, (side - 1) * key_rows)], flat_send.at[0])
    drain(vbuf.at[:, 0, pl.ds(0, (side - 1) * key_rows)], flat_send.at[1])
    drain(qbuf.at[pl.ds(0, heads), others], flat_send.at[2])

    @pl.when(is_mid)
    def _():
        for i, buf in enumerate((kbuf, vbuf)):
            drain(buf.at[:, pl.ds(0, 2)], line_send.at[0, i])
            drain(buf.at[pl.ds(0, near), pl.ds(0, 3)], line_send.at[1, i])
        drain(obuf.at[pl.ds(0, heads), 0], o_home)
        drain(obuf.at[pl.ds(0, heads), others], o_send.at[0])
        drain(obuf.at[pl.ds(0, far)], o_send.at[1])
        drain(obuf.at[pl.ds(0, heads), others], o_recv.at[0])

    @pl.when(is_edge)
    def _():
        for i, buf in enumerate((kbuf, vbuf)):
            drain(buf.at[:, 0], line_send.at[1, i])
        drain(qbuf.at[pl.ds(0, far)], far_send)
        drain(obuf.at[pl.ds(0, near), 0], o_home)
        drain(obuf.at[pl.ds(0, near), others], o_send.at[0])
        drain(obuf.at[pl.ds(0, near), others], o_recv.at[0])
        drain(obuf.at[pl.ds(0, far)], o_recv.at[1])


def flagged(lists, counts, key_blocks):
    listed = lists.shape[2]
    usable = jnp.arange(listed, dtype=jnp.int32) < counts[:, :, None]
    chosen = jnp.where(usable, lists, -1)
    flags = -(-key_blocks // HEAD_DIM) * HEAD_DIM
    blocks = jnp.arange(flags, dtype=jnp.int32)
    member = jnp.any(chosen[:, :, :, None] == blocks, axis=2)
    return jnp.where(member, 0.0, NEGATIVE).astype(jnp.float32)


LINE = 4
CORES = 2


def shared_heads(heads):
    return [2] + list(range(4, heads))


def fits_line(blk_n, uly_n, heads_all, rows):
    side = blk_n // LINE * uly_n
    return (
        blk_n == LINE * 2 * CORES and uly_n == 2
        and heads_all % side == 0 and 5 <= heads_all // side <= 6
        and rows % BLOCK == 0
    )


def along_line(blk_n, uly_n, queries, keys, values, block_lists, block_counts):
    heads_all, qblocks_all, listed = block_lists.shape
    devices, planes = blk_n * uly_n, LINE
    per_blk = blk_n // planes
    side = per_blk * uly_n
    heads = heads_all // side
    slots = heads + len(shared_heads(heads))
    rows, key_rows = queries.shape[0], keys.shape[0]
    keys_all = key_rows * devices
    flags = -(-(keys_all // BLOCK) // HEAD_DIM) * HEAD_DIM

    any_spec = pl.BlockSpec(memory_space=pl.ANY)
    dma = pltpu.SemaphoreType.DMA
    plane_keys = side * key_rows
    return pl.pallas_call(
        functools.partial(line_kernel, planes, per_blk, uly_n),
        out_shape=jax.ShapeDtypeStruct(queries.shape, queries.dtype),
        in_specs=[any_spec] * 5,
        out_specs=any_spec,
        scratch_shapes=[
            pltpu.VMEM((slots, side, rows, HEAD_DIM), jnp.bfloat16),
            pltpu.VMEM((heads, planes, plane_keys, HEAD_DIM), jnp.bfloat16),
            pltpu.VMEM((heads, planes, plane_keys, HEAD_DIM), jnp.bfloat16),
            pltpu.VMEM((slots, side, rows, HEAD_DIM), jnp.bfloat16),
            pltpu.VMEM((keys_all, flags), jnp.bfloat16),
            pltpu.VMEM((heads, qblocks_all, flags), jnp.float32),
            pltpu.VMEM((heads, listed, qblocks_all), jnp.int32),
            pltpu.VMEM((heads_all, qblocks_all), jnp.int32),
            pltpu.VMEM((2, rows, keys_all), jnp.float32),
            pltpu.VMEM((2, rows, HEAD_DIM), jnp.float32),
            dma((heads,)), dma((heads,)), dma((heads,)),
            dma((heads, planes)), dma((heads, planes)), dma((slots - heads,)),
            dma((3,)), dma((2, 2)), dma, dma((2,)), dma((2,)), dma, dma((2,)),
        ],
        compiler_params=pltpu.CompilerParams(
            collective_id=1, has_side_effects=True, vmem_limit_bytes=40 * 1024 * 1024
        ),
    )(*(pltpu.with_memory_space_constraint(a, pltpu.HBM) for a in (queries, keys, values, jnp.swapaxes(block_lists, 1, 2), block_counts)))


def local(blk_n, uly_n, queries, keys, values, block_lists, block_counts):
    heads_all, qblocks_all, listed = block_lists.shape
    if fits_line(blk_n, uly_n, heads_all, queries.shape[0]):
        return along_line(blk_n, uly_n, queries, keys, values, block_lists, block_counts)
    share = math.gcd(blk_n, heads_all // uly_n)
    group = share * uly_n
    heads = heads_all // group
    groups = blk_n // share
    qblocks = qblocks_all // groups
    devices = blk_n * uly_n
    rows, key_rows = queries.shape[0], keys.shape[0]
    width = heads * HEAD_DIM
    keys_all = key_rows * devices

    me = lax.axis_index("blk") * uly_n + lax.axis_index("uly")
    place = lax.rem(me, group)
    lists = lax.dynamic_slice(
        block_lists, (place * heads, (me // group) * qblocks, 0), (heads, qblocks, listed)
    )
    counts = lax.dynamic_slice(
        block_counts, (place * heads, (me // group) * qblocks), (heads, qblocks)
    )
    bias = flagged(lists, counts, keys_all // BLOCK)
    flags = bias.shape[2]

    any_spec = pl.BlockSpec(memory_space=pl.ANY)
    dma = pltpu.SemaphoreType.DMA
    return pl.pallas_call(
        functools.partial(attend_kernel, blk_n, uly_n, group),
        out_shape=jax.ShapeDtypeStruct(queries.shape, queries.dtype),
        in_specs=[any_spec, any_spec, any_spec, pl.BlockSpec(memory_space=pltpu.VMEM)],
        out_specs=any_spec,
        scratch_shapes=[
            pltpu.VMEM((group, rows, width), jnp.bfloat16),
            pltpu.VMEM((devices, key_rows, width), jnp.bfloat16),
            pltpu.VMEM((devices, key_rows, width), jnp.bfloat16),
            pltpu.VMEM((group, rows, width), jnp.bfloat16),
            pltpu.VMEM((keys_all, flags), jnp.bfloat16),
            dma((2,)), dma, dma, dma, dma((group,)), dma, dma, dma((4,)),
        ],
        compiler_params=pltpu.CompilerParams(
            collective_id=0, has_side_effects=True, vmem_limit_bytes=60 * 1024 * 1024
        ),
    )(queries, keys, values, bias)


def solution(mesh):
    return jax.shard_map(
        functools.partial(local, mesh.shape["blk"], mesh.shape["uly"]),
        mesh=mesh,
        in_specs=(
            P(("blk", "uly"), None),
            P(("blk", "uly"), None),
            P(("blk", "uly"), None),
            P(),
            P(),
        ),
        out_specs=P(("blk", "uly"), None),
        check_vma=False,
    )
```
